1024 devices in a mesh: pipe: 8 (over y), seq: 16 (over z, core), head: 8 (over x).
Axes of the slice: x: 8, y: 8, z: 8, core: 2. Of those that a mesh axis runs over, the one named last changes fastest.
Arguments:
- queries: bfloat16 [8, 4096, 4096], P('pipe', 'seq', 'head'), may hold values from -6 to 6
- keys: bfloat16 [8, 4096, 4096], P('pipe', 'seq', 'head'), may hold values from -6 to 6
- values: bfloat16 [8, 4096, 4096], P('pipe', 'seq', 'head'), may hold values from -6 to 6
- output_gradient: bfloat16 [8, 4096, 4096], P('pipe', 'seq', 'head'), may hold values from -0.019897461 to 0.019897461
- log_decay: float32 [8, 32, 4096], P('pipe', 'head', 'seq'), may hold values from -1.5 to 0
Outputs:
- query_grad_in: bfloat16 [8, 4096, 4096], P('pipe', 'seq', 'head')
- key_grad_in: bfloat16 [8, 4096, 4096], P('pipe', 'seq', 'head')
- value_grad_in: bfloat16 [8, 4096, 4096], P('pipe', 'seq', 'head')
The draws below stay inside these ranges and needn't reach their ends.
All inputs are finite; a program needn't handle non-finite values.
Results may differ from the reference program's by a relative error of at most 0.0057.
Values may be sent and summed in bfloat16 or wider, within the bound.
A program may use at most 32 MiB of HBM per device.

```python
import math
import jax
import jax.numpy as jnp
from jax import lax

HEADS = 32
HEAD_DIM = 128
TOK_DEV = 256
SEQ = 4096
SECTIONS = 8
FEATURES = 4096
N_SEQ = 16


def draw_log_decay(key, part):
    streams = jax.random.split(key, 7)
    fast_share = 0.5
    fast = jax.random.bernoulli(streams[0], fast_share, (SECTIONS, HEADS, 1))
    slow_total = jnp.exp(jax.random.uniform(streams[1], (SECTIONS, HEADS, 1), jnp.float32, math.log(0.1), math.log(0.5)))
    fast_rate = jnp.exp(jax.random.uniform(streams[2], (SECTIONS, HEADS, 1), jnp.float32, math.log(0.05), math.log(0.1)))
    fading_speed = jnp.where(fast, fast_rate, slow_total / SEQ)
    blocks = SEQ // TOK_DEV
    processor_scale_factor = jnp.exp(jax.random.uniform(streams[3], (SECTIONS, HEADS, blocks, 1), jnp.float32, math.log(0.5), math.log(2.0)))
    processor_scale_factor = jnp.broadcast_to(processor_scale_factor, (SECTIONS, HEADS, blocks, TOK_DEV)).reshape(SECTIONS, HEADS, SEQ)
    index_scale_factor = jnp.exp(jax.random.uniform(streams[4], (SECTIONS, HEADS, SEQ), jnp.float32, -0.5, 0.5))
    location_sequence = jax.random.randint(streams[5], (SECTIONS, HEADS, 2, 1), 0, SEQ)
    objective_numbers = jax.random.uniform(streams[6], (SECTIONS, HEADS, 2, 1), jnp.float32, math.log(0.6), math.log(0.8))
    point_sequence = jnp.arange(SEQ, dtype=jnp.int32)[None, None, None, :]
    segment_bundles = jnp.sum(jnp.where(point_sequence == location_sequence, objective_numbers, 0.0), axis=2)
    return (-fading_speed * processor_scale_factor * index_scale_factor + segment_bundles).astype(jnp.float32)


def levels(stream_key, extent, cuts, smallest, top_value):
    loudness = 1.0
    for dim, shards_of in cuts:
        heights = jax.random.uniform(jax.random.fold_in(jax.random.fold_in(stream_key, 6), dim), (shards_of,), jnp.float32, smallest / len(cuts), top_value / len(cuts))
        loudness = loudness * jnp.repeat(jnp.exp(heights), extent[dim] // shards_of).reshape((-1,) + (1,) * (len(extent) - 1 - dim))
    return loudness


def centred(rng, extent, scale, most, cuts=(), kind=jnp.bfloat16):
    result = jax.random.normal(rng, extent, jnp.float32) * scale
    if len(cuts) > 0:
        result = levels(rng, extent, cuts, -0.22, 0.18) * result
    return jnp.clip(result, min=-most, max=most).astype(kind)


def setup_inputs(seed: int = 0) -> dict:
    arg_keys = jax.random.split(jax.random.key(seed), 6)
    queries = centred(arg_keys[0], (SECTIONS, SEQ, FEATURES), 1.0, 6.0, ((0, 8), (1, 16), (2, 8)))
    keys = centred(arg_keys[1], (SECTIONS, SEQ, FEATURES), 1.0, 6.0, ((0, 8), (1, 16), (2, 8)))
    values = centred(arg_keys[2], (SECTIONS, SEQ, FEATURES), 1.0, 6.0, ((0, 8), (1, 16), (2, 8)))
    output_gradient = centred(arg_keys[3], (SECTIONS, SEQ, FEATURES), 0.003, 0.019897461, ((0, 8), (1, 16), (2, 8)))
    log_decay = draw_log_decay(jax.random.fold_in(arg_keys[5], 71), 0)
    return {"queries": queries, "keys": keys, "values": values, "output_gradient": output_gradient, "log_decay": log_decay}


def segment_states(queries, keys, values, output_gradient, cum):
    total = cum[:, -1]
    scaled_keys = (jnp.exp(total[:, None] - cum)[..., None] * keys.astype(jnp.float32)).astype(jnp.bfloat16)
    scaled_queries = (jnp.exp(cum)[..., None] * queries.astype(jnp.float32)).astype(jnp.bfloat16)
    local_forward_state = jnp.einsum('nwd,nws->nds', scaled_keys.astype(jnp.float32), values.astype(jnp.float32))
    local_reverse_state = jnp.einsum('nwd,nws->nds', scaled_queries.astype(jnp.float32), output_gradient.astype(jnp.float32))
    return total, local_forward_state, local_reverse_state


def head_grads(inputs):
    queries, keys, values, output_gradient, cum, total, state_in, state_rev = inputs
    count = cum.shape[0]
    later = lax.broadcasted_iota(jnp.int32, (count, count), 0) >= lax.broadcasted_iota(jnp.int32, (count, count), 1)
    decay = jnp.where(later, jnp.exp(jnp.where(later, cum[:, None] - cum[None, :], 0.0)), 0.0)
    inner = (((1,), (1,)), ((), ()))
    outer = (((0,), (0,)), ((), ()))
    pair = (lax.dot_general(output_gradient, values, inner, preferred_element_type=jnp.float32) * decay).astype(jnp.bfloat16)
    score = (lax.dot_general(queries, keys, inner, preferred_element_type=jnp.float32) * decay).astype(jnp.bfloat16)
    forward_b = state_in.astype(jnp.bfloat16)
    reverse_b = state_rev.astype(jnp.bfloat16)
    lead = jnp.exp(cum)[:, None]
    tail = jnp.exp(total - cum)[:, None]
    query_grad = jnp.dot(pair, keys, preferred_element_type=jnp.float32) + lead * lax.dot_general(output_gradient, forward_b, inner, preferred_element_type=jnp.float32)
    key_grad = lax.dot_general(pair, queries, outer, preferred_element_type=jnp.float32) + tail * lax.dot_general(values, reverse_b, inner, preferred_element_type=jnp.float32)
    value_grad = lax.dot_general(score, output_gradient, outer, preferred_element_type=jnp.float32) + tail * jnp.dot(keys, reverse_b, preferred_element_type=jnp.float32)
    return query_grad.astype(jnp.bfloat16), key_grad.astype(jnp.bfloat16), value_grad.astype(jnp.bfloat16)


def section_grads(inputs):
    queries, keys, values, output_gradient, log_decay = inputs

    def split(array):
        return array.reshape(N_SEQ, TOK_DEV, HEADS, HEAD_DIM).transpose(0, 2, 1, 3)

    parts = (split(queries), split(keys), split(values), split(output_gradient))
    cum = jnp.cumsum(log_decay.reshape(HEADS, N_SEQ, TOK_DEV).transpose(1, 0, 2), axis=2)
    totals, forward, reverse = lax.map(lambda items: segment_states(*items), parts + (cum,))
    zeros = jnp.zeros((HEADS, HEAD_DIM, HEAD_DIM), jnp.float32)

    def advance(carry, items):
        return jnp.exp(items[0])[:, None, None] * carry + items[1], carry

    unused, state_in = lax.scan(advance, zeros, (totals, forward))
    unused, state_rev = lax.scan(advance, zeros, (totals, reverse), reverse=True)

    def segment_grads(items):
        return lax.map(head_grads, items)

    query_grad, key_grad, value_grad = lax.map(segment_grads, parts + (cum, totals, state_in, state_rev))

    def merge(array):
        return array.transpose(0, 2, 1, 3).reshape(SEQ, FEATURES)

    return merge(query_grad), merge(key_grad), merge(value_grad)


def reference(queries, keys, values, output_gradient, log_decay):
    query_grad, key_grad, value_grad = lax.map(section_grads, (queries, keys, values, output_gradient, log_decay))

    def passed(array):
        return jnp.concatenate([array[1:], jnp.zeros_like(array[:1])], axis=0)

    return passed(query_grad), passed(key_grad), passed(value_grad)
```

```python
import functools

import jax
import jax.numpy as jnp
from jax import lax
from jax.experimental import pallas as pl
from jax.experimental.pallas import tpu as pltpu
from jax.sharding import PartitionSpec as P

MESH = pl.DeviceIdType.MESH
INNER = (((1,), (1,)), ((), ()))
OUTER = (((0,), (0,)), ((), ()))
F32 = jnp.float32
BF16 = jnp.bfloat16


def mm(a, b):
    return jnp.dot(a, b, preferred_element_type=F32)


def mm_nt(a, b):
    return lax.dot_general(a, b, INNER, preferred_element_type=F32)


def mm_tn(a, b):
    return lax.dot_general(a, b, OUTER, preferred_element_type=F32)


def far_first(count):
    ring = count + 1
    return sorted(range(1, count + 1), key=lambda d: -min(d, ring - d))


def kernel(
    n_pipe,
    n_chip,
    q_hbm,
    k_hbm,
    v_hbm,
    g_hbm,
    ld_hbm,
    oq_ref,
    ok_ref,
    ov_ref,
    q_ref,
    k_ref,
    v_ref,
    g_ref,
    ld_ref,
    part_ref,
    cum_ref,
    col_ref,
    lead_ref,
    tail_ref,
    tot_ref,
    tot_sib_ref,
    chip_tot_ref,
    far_tot_ref,
    weight_ref,
    local_ref,
    sib_state_ref,
    agg_ref,
    far_ref,
    own_ref,
    sib_sum_ref,
    state_ref,
    iq_ref,
    ik_ref,
    iv_ref,
    out_ref,
    zero_ref,
    in_sem,
    tot_send,
    tot_recv,
    x_send,
    x_recv,
    ft_send,
    ft_recv,
    agg_send,
    agg_recv,
    u_send,
    u_recv,
    y_send,
    y_recv,
    zero_sem,
):
    length, width = q_ref.shape
    heads = ld_ref.shape[1]
    size = width // heads
    half = length // 2
    n_far = n_chip - 1

    pipe = lax.axis_index("pipe")
    seq = lax.axis_index("seq")
    chip = lax.div(seq, 2)
    core = lax.rem(seq, 2)
    sibling = seq + 1 - 2 * core
    step = 2 * core - 1
    n_partner = core * (n_far - chip) + (1 - core) * chip
    below = lax.rem(pipe + n_pipe - 1, n_pipe)
    above = lax.rem(pipe + 1, n_pipe)

    def partner(d):
        return 2 * (chip + step * d) + (1 - core)

    barrier = pltpu.get_barrier_semaphore()
    pl.semaphore_signal(barrier, inc=1, device_id={"seq": sibling}, device_id_type=MESH)
    for d in far_first(n_far):

        @pl.when(d <= n_partner)
        def _():
            pl.semaphore_signal(barrier, inc=1, device_id={"seq": partner(d)}, device_id_type=MESH)

    @pl.when(pipe < n_pipe - 1)
    def _():
        pl.semaphore_signal(barrier, inc=1, device_id={"pipe": above}, device_id_type=MESH)

    loads = [
        pltpu.make_async_copy(ld_hbm, ld_ref, in_sem.at[0]),
        pltpu.make_async_copy(k_hbm.at[0], k_ref, in_sem.at[1]),
        pltpu.make_async_copy(v_hbm.at[0], v_ref, in_sem.at[2]),
        pltpu.make_async_copy(q_hbm.at[0], q_ref, in_sem.at[3]),
        pltpu.make_async_copy(g_hbm.at[0], g_ref, in_sem.at[4]),
    ]
    for load in loads:
        load.start()

    for d in range(1, n_far + 1):

        @pl.when(d > n_partner)
        def _():
            far_ref[d - 1] = jnp.zeros(far_ref.shape[1:], BF16)
            far_tot_ref[d - 1] = jnp.zeros(far_tot_ref.shape[1:], F32)

    part_ref[...] = jnp.zeros_like(part_ref)
    cum_ref[...] = jnp.zeros_like(cum_ref)

    @pl.when(pipe == n_pipe - 1)
    def _():
        zero_ref[...] = jnp.zeros_like(zero_ref)
        clears = [
            pltpu.make_async_copy(zero_ref, o.at[0], zero_sem.at[i])
            for i, o in enumerate((oq_ref, ok_ref, ov_ref))
        ]
        for clear in clears:
            clear.start()
        for clear in clears:
            clear.wait()

    loads[0].wait()
    ld = ld_ref[0]
    high = ld.astype(BF16).astype(F32)
    rest = ld - high
    middle = rest.astype(BF16).astype(F32)
    part_ref[0:heads, :] = high
    part_ref[heads : 2 * heads, :] = middle
    part_ref[2 * heads : 3 * heads, :] = rest - middle
    earlier = (
        lax.broadcasted_iota(jnp.int32, (length, length), 0)
        <= lax.broadcasted_iota(jnp.int32, (length, length), 1)
    ).astype(F32).astype(BF16)
    sums = mm(part_ref[...].astype(BF16), earlier)
    cum_ref[0:heads, :] = sums[0:heads] + sums[heads : 2 * heads] + sums[2 * heads : 3 * heads]
    tot_ref[...] = jnp.broadcast_to(cum_ref[:, length - 1 : length], tot_ref.shape)

    for load in loads[1:]:
        load.wait()

    def cols(ref, h):
        return ref[:, h * size : (h + 1) * size]

    for h in range(heads):
        for b in range(2):
            rows = slice(b * half, (b + 1) * half)
            row = jnp.broadcast_to(cum_ref[h : h + 1, rows], (half, half))
            col_ref[h, rows, :] = row.T
        col = col_ref[h]
        lead = jnp.exp(col)
        tail = jnp.exp(tot_ref[h : h + 1, :] - col)
        lead_ref[h] = lead
        tail_ref[h] = tail
        key_weighted = (tail * cols(k_ref, h).astype(F32)).astype(BF16)
        query_weighted = (lead * cols(q_ref, h).astype(F32)).astype(BF16)
        local_ref[0, h] = mm_tn(key_weighted, cols(v_ref, h))
        local_ref[1, h] = mm_tn(query_weighted, cols(g_ref, h))
        if h == 0:
            pl.semaphore_wait(barrier, 1 + n_partner + jnp.minimum(pipe, 1))
            tot_copy = pltpu.make_async_remote_copy(
                src_ref=tot_ref,
                dst_ref=tot_sib_ref,
                send_sem=tot_send.at[0],
                recv_sem=tot_recv.at[0],
                device_id={"seq": sibling},
                device_id_type=MESH,
            )
            tot_copy.start()
        x_copy(local_ref, sib_state_ref, core, h, x_send, x_recv, sibling).start()

    def tot_far(d):
        return pltpu.make_async_remote_copy(
            src_ref=chip_tot_ref,
            dst_ref=far_tot_ref.at[d - 1],
            send_sem=ft_send.at[d - 1],
            recv_sem=ft_recv.at[d - 1],
            device_id={"seq": partner(d)},
            device_id_type=MESH,
        )

    def agg_far(d, h):
        return pltpu.make_async_remote_copy(
            src_ref=agg_ref.at[h],
            dst_ref=far_ref.at[d - 1, h],
            send_sem=agg_send.at[d - 1, h],
            recv_sem=agg_recv.at[d - 1, h],
            device_id={"seq": partner(d)},
            device_id_type=MESH,
        )

    tot_copy.wait_recv()
    chip_tot_ref[...] = tot_ref[...] + tot_sib_ref[...]
    for d in far_first(n_far):

        @pl.when(d <= n_partner)
        def _():
            tot_far(d).start()

    for h in range(heads):
        x_copy(local_ref, sib_state_ref, core, h, x_send, x_recv, sibling).wait_recv()
        agg_ref[h] = (
            jnp.exp(tot_ref[h : h + 1, :]) * sib_state_ref[h] + local_ref[1 - core, h]
        ).astype(BF16)
        for d in far_first(n_far):

            @pl.when(d <= n_partner)
            def _():
                agg_far(d, h).start()

    at = lax.broadcasted_iota(jnp.int32, (half, half), 0)
    by = lax.broadcasted_iota(jnp.int32, (half, half), 1)
    lower, upper = at >= by, at <= by
    for h in range(heads):
        q, k, v, g = cols(q_ref, h), cols(k_ref, h), cols(v_ref, h), cols(g_ref, h)
        row0, row1 = cum_ref[h : h + 1, :half], cum_ref[h : h + 1, half:]
        col0, col1 = col_ref[h, :half, :], col_ref[h, half:, :]
        d00 = jnp.where(lower, jnp.exp(col0 - row0), 0.0)
        d10 = jnp.exp(col1 - row0)
        d11 = jnp.where(lower, jnp.exp(col1 - row1), 0.0)
        pair0 = (mm_nt(g[:half], v[:half]) * d00).astype(BF16)
        pair1 = (mm_nt(g[half:], v) * jnp.concatenate([d10, d11], axis=1)).astype(BF16)
        iq_ref[h, :half, :] = mm(pair0, k[:half])
        iq_ref[h, half:, :] = mm(pair1, k)
        e00 = jnp.where(upper, jnp.exp(row0 - col0), 0.0)
        e01 = jnp.exp(row1 - col0)
        e11 = jnp.where(upper, jnp.exp(row1 - col1), 0.0)
        e0 = jnp.concatenate([e00, e01], axis=1)
        pair_t0 = (mm_nt(v[:half], g) * e0).astype(BF16)
        pair_t1 = (mm_nt(v[half:], g[half:]) * e11).astype(BF16)
        ik_ref[h, :half, :] = mm(pair_t0, q)
        ik_ref[h, half:, :] = mm(pair_t1, q[half:])
        score_t0 = (mm_nt(k[:half], q) * e0).astype(BF16)
        score_t1 = (mm_nt(k[half:], q[half:]) * e11).astype(BF16)
        iv_ref[h, :half, :] = mm(score_t0, g)
        iv_ref[h, half:, :] = mm(score_t1, g[half:])

    between = jnp.zeros(tot_ref.shape, F32)
    for d in range(1, n_far + 1):

        @pl.when(d <= n_partner)
        def _():
            tot_far(d).wait_recv()

        weight_ref[d - 1] = jnp.exp(between)
        between = between + far_tot_ref[d - 1]

    def u_copy(h):
        return pltpu.make_async_remote_copy(
            src_ref=own_ref.at[h],
            dst_ref=sib_sum_ref.at[h],
            send_sem=u_send.at[h],
            recv_sem=u_recv.at[h],
            device_id={"seq": sibling},
            device_id_type=MESH,
        )

    outs = (oq_ref, ok_ref, ov_ref)

    def y_copy(j, h):
        return pltpu.make_async_remote_copy(
            src_ref=out_ref.at[j, h],
            dst_ref=outs[j].at[0, :, pl.ds(h * size, size)],
            send_sem=y_send.at[j, h],
            recv_sem=y_recv.at[j, h],
            device_id={"pipe": below},
            device_id_type=MESH,
        )

    def send_down(j, h):
        @pl.when(pipe > 0)
        def _():
            y_copy(j, h).start()

    for h in range(heads):
        for d in range(1, n_far + 1):

            @pl.when(d <= n_partner)
            def _():
                agg_far(d, h).wait_recv()

        total = jnp.zeros((size, size), F32)
        for d in range(1, n_far + 1):
            total = total + weight_ref[d - 1, h : h + 1, :] * far_ref[d - 1, h].astype(F32)
        own_ref[h] = total
        u_copy(h).start()
        state_ref[core, h] = total.astype(BF16)
        u_copy(h).wait_recv()
        state_ref[1 - core, h] = (
            jnp.exp(tot_sib_ref[h : h + 1, :]) * sib_sum_ref[h] + sib_state_ref[h]
        ).astype(BF16)
        state_in, state_rev = state_ref[0, h], state_ref[1, h]
        lead, tail = lead_ref[h], tail_ref[h]
        out_ref[0, h] = (iq_ref[h] + lead * mm_nt(cols(g_ref, h), state_in)).astype(BF16)
        send_down(0, h)
        out_ref[1, h] = (ik_ref[h] + tail * mm_nt(cols(v_ref, h), state_rev)).astype(BF16)
        send_down(1, h)
        out_ref[2, h] = (iv_ref[h] + tail * mm(cols(k_ref, h), state_rev)).astype(BF16)
        send_down(2, h)

    tot_copy.wait_send()
    for h in range(heads):
        x_copy(local_ref, sib_state_ref, core, h, x_send, x_recv, sibling).wait_send()
        u_copy(h).wait_send()
    for d in range(1, n_far + 1):

        @pl.when(d <= n_partner)
        def _():
            tot_far(d).wait_send()
            for h in range(heads):
                agg_far(d, h).wait_send()

    @pl.when(pipe > 0)
    def _():
        for h in range(heads):
            for j in range(3):
                y_copy(j, h).wait_send()

    @pl.when(pipe < n_pipe - 1)
    def _():
        for h in range(heads):
            for j in range(3):
                y_copy(j, h).wait_recv()


def x_copy(local_ref, sib_state_ref, core, h, x_send, x_recv, sibling):
    return pltpu.make_async_remote_copy(
        src_ref=local_ref.at[core, h],
        dst_ref=sib_state_ref.at[h],
        send_sem=x_send.at[h],
        recv_sem=x_recv.at[h],
        device_id={"seq": sibling},
        device_id_type=MESH,
    )


def per_device(n_pipe, n_seq, queries, keys, values, output_gradient, log_decay):
    length, width = queries.shape[1:]
    heads = log_decay.shape[1]
    size = width // heads
    n_chip = n_seq // 2
    n_far = n_chip - 1
    dma = pltpu.SemaphoreType.DMA
    tile = (8, size)
    anywhere = pl.BlockSpec(memory_space=pl.ANY)
    return pl.pallas_call(
        functools.partial(kernel, n_pipe, n_chip),
        out_shape=[jax.ShapeDtypeStruct(queries.shape, BF16)] * 3,
        in_specs=[anywhere] * 5,
        out_specs=[anywhere] * 3,
        scratch_shapes=[
            *[pltpu.VMEM((length, width), BF16)] * 4,
            pltpu.VMEM((1, heads, length), F32),
            pltpu.VMEM((16, length), F32),
            pltpu.VMEM((8, length), F32),
            *[pltpu.VMEM((heads, length, size), F32)] * 3,
            *[pltpu.VMEM(tile, F32)] * 3,
            *[pltpu.VMEM((n_far, *tile), F32)] * 2,
            pltpu.VMEM((2, heads, size, size), F32),
            pltpu.VMEM((heads, size, size), F32),
            pltpu.VMEM((heads, size, size), BF16),
            pltpu.VMEM((n_far, heads, size, size), BF16),
            *[pltpu.VMEM((heads, size, size), F32)] * 2,
            pltpu.VMEM((2, heads, size, size), BF16),
            *[pltpu.VMEM((heads, length, size), F32)] * 3,
            pltpu.VMEM((3, heads, length, size), BF16),
            pltpu.VMEM((length, width), BF16),
            dma((5,)),
            dma((1,)),
            dma((1,)),
            dma((heads,)),
            dma((heads,)),
            dma((n_far,)),
            dma((n_far,)),
            dma((n_far, heads)),
            dma((n_far, heads)),
            dma((heads,)),
            dma((heads,)),
            dma((3, heads)),
            dma((3, heads)),
            dma((3,)),
        ],
        compiler_params=pltpu.CompilerParams(collective_id=0, has_side_effects=True),
    )(queries, keys, values, output_gradient, log_decay)


def solution(mesh):
    in_specs = (
        P("pipe", "seq", "head"),
        P("pipe", "seq", "head"),
        P("pipe", "seq", "head"),
        P("pipe", "seq", "head"),
        P("pipe", "head", "seq"),
    )
    out_specs = (P("pipe", "seq", "head"), P("pipe", "seq", "head"), P("pipe", "seq", "head"))
    body = functools.partial(per_device, mesh.shape["pipe"], mesh.shape["seq"])
    return jax.shard_map(body, mesh=mesh, in_specs=in_specs, out_specs=out_specs, check_vma=False)
```

```python
import functools

import jax
import jax.numpy as jnp
from jax import lax
from jax.experimental import pallas as pl
from jax.experimental.pallas import tpu as pltpu
from jax.sharding import PartitionSpec as P

MESH = pl.DeviceIdType.MESH
INNER = (((1,), (1,)), ((), ()))
OUTER = (((0,), (0,)), ((), ()))
F32 = jnp.float32
BF16 = jnp.bfloat16


def mm(a, b):
    return jnp.dot(a, b, preferred_element_type=F32)


def mm_nt(a, b):
    return lax.dot_general(a, b, INNER, preferred_element_type=F32)


def mm_tn(a, b):
    return lax.dot_general(a, b, OUTER, preferred_element_type=F32)


def running_sums(ld, part_ref, cum_ref, tot_ref):
    heads, length = ld.shape
    high = ld.astype(BF16).astype(F32)
    rest = ld - high
    middle = rest.astype(BF16).astype(F32)
    part_ref[0:heads, :] = high
    part_ref[heads : 2 * heads, :] = middle
    part_ref[2 * heads : 3 * heads, :] = rest - middle
    earlier = (
        (
            lax.broadcasted_iota(jnp.int32, (length, length), 0)
            <= lax.broadcasted_iota(jnp.int32, (length, length), 1)
        )
        .astype(F32)
        .astype(BF16)
    )
    sums = mm(part_ref[...].astype(BF16), earlier)
    cum_ref[0:heads, :] = sums[0:heads] + sums[heads : 2 * heads] + sums[2 * heads : 3 * heads]
    tot_ref[...] = jnp.broadcast_to(cum_ref[:, length - 1 : length], tot_ref.shape)


def as_columns(cum_ref, h, half):
    blocks = []
    for b in range(2):
        row = cum_ref[h : h + 1, b * half : (b + 1) * half]
        blocks.append(jnp.broadcast_to(row, (half, half)).T)
    return jnp.concatenate(blocks, axis=0)


def kernel(
    n_pipe,
    n_chip,
    q_hbm,
    k_hbm,
    v_hbm,
    g_hbm,
    ld_hbm,
    oq_ref,
    ok_ref,
    ov_ref,
    q_ref,
    k_ref,
    v_ref,
    g_ref,
    ld_ref,
    part_ref,
    cum_ref,
    tot_ref,
    tot_sib_ref,
    chip_tot_ref,
    far_tot_ref,
    weight_ref,
    tail_ref,
    local_ref,
    sib_state_ref,
    agg_ref,
    far_ref,
    ship_ref,
    up_ref,
    up_ld_ref,
    up_state_ref,
    up_cum_ref,
    up_tot_ref,
    up_lead_ref,
    up_tail_ref,
    iq_ref,
    ik_ref,
    iv_ref,
    in_sem,
    tot_send,
    tot_recv,
    x_send,
    x_recv,
    ft_send,
    ft_recv,
    agg_send,
    agg_recv,
    ld_send,
    ld_recv,
    y_send,
    y_recv,
    st_send,
    st_recv,
    ready,
    low_ready,
    cross_ready,
):
    length, width = q_ref.shape
    heads = ld_ref.shape[1]
    size = width // heads
    half = length // 2
    n_far = n_chip - 1

    pipe = lax.axis_index("pipe")
    seq = lax.axis_index("seq")
    chip = lax.div(seq, 2)
    core = lax.rem(seq, 2)
    sibling = seq + 1 - 2 * core
    step = 2 * core - 1
    n_partner = core * (n_far - chip) + (1 - core) * chip
    below = lax.rem(pipe + n_pipe - 1, n_pipe)
    above = lax.rem(pipe + 1, n_pipe)
    is_source = pipe > 0
    is_target = pipe < n_pipe - 1

    def partner(d):
        return 2 * (chip + step * d) + (1 - core)

    def cols(ref, h):
        return ref[:, h * size : (h + 1) * size]

    def remote(src, dst, send, recv, device):
        return pltpu.make_async_remote_copy(
            src_ref=src,
            dst_ref=dst,
            send_sem=send,
            recv_sem=recv,
            device_id=device,
            device_id_type=MESH,
        )

    def signal(sem, device):
        pl.semaphore_signal(sem, inc=1, device_id=device, device_id_type=MESH)

    inputs = (q_hbm, g_hbm, k_hbm, v_hbm)
    held = (q_ref, g_ref, k_ref, v_ref)

    def tot_copy():
        return remote(tot_ref, tot_sib_ref, tot_send.at[0], tot_recv.at[0], {"seq": sibling})

    def x_copy(h):
        return remote(
            local_ref.at[core, h], sib_state_ref.at[h], x_send.at[h], x_recv.at[h], {"seq": sibling}
        )

    def tot_far(d):
        return remote(
            chip_tot_ref,
            far_tot_ref.at[d - 1],
            ft_send.at[d - 1],
            ft_recv.at[d - 1],
            {"seq": partner(d)},
        )

    def agg_far(d, h):
        return remote(
            agg_ref.at[h],
            far_ref.at[d - 1, h],
            agg_send.at[d - 1, h],
            agg_recv.at[d - 1, h],
            {"seq": partner(d)},
        )

    def ld_copy():
        return remote(ld_ref, up_ld_ref, ld_send.at[0], ld_recv.at[0], {"pipe": below})

    def y_copy(i, h):
        return remote(
            held[i].at[:, pl.ds(h * size, size)],
            up_ref.at[i, h],
            y_send.at[i, h],
            y_recv.at[i, h],
            {"pipe": below},
        )

    def st_copy(other, h):
        device = {"pipe": below, "seq": sibling if other else seq}
        return remote(
            ship_ref.at[other, h],
            up_state_ref.at[core, h],
            st_send.at[other, h],
            st_recv.at[core, h],
            device,
        )

    barrier = pltpu.get_barrier_semaphore()
    busy = jnp.minimum(pipe, 1)

    @pl.when(is_source)
    def _():
        signal(barrier, {"seq": sibling})

    @pl.when(pipe == 1)
    def _():
        signal(barrier, {"pipe": below})

    @pl.when(jnp.logical_and(is_source, is_target))
    def _():
        signal(barrier, {"pipe": above})

    loads = [pltpu.make_async_copy(ld_hbm, ld_ref, in_sem.at[4])]
    for i, (src, dst) in enumerate(zip(inputs, held)):
        loads.append(pltpu.make_async_copy(src.at[0], dst, in_sem.at[i]))
    @pl.when(is_source)
    def _():
        for load in loads:
            load.start()

    for d in range(1, n_far + 1):

        @pl.when(d > n_partner)
        def _():
            far_ref[d - 1] = jnp.zeros(far_ref.shape[1:], BF16)
            far_tot_ref[d - 1] = jnp.zeros(far_tot_ref.shape[1:], F32)

    part_ref[...] = jnp.zeros_like(part_ref)
    cum_ref[...] = jnp.zeros_like(cum_ref)
    up_cum_ref[...] = jnp.zeros_like(up_cum_ref)

    pl.semaphore_wait(barrier, 1 + busy * jnp.minimum(chip, 1) + jnp.minimum(lax.div(pipe, 2), 1))

    @pl.when(jnp.logical_and(is_source, chip < n_far))
    def _():
        signal(barrier, {"seq": seq + 2})

    @pl.when(pipe == 0)
    def _():
        signal(low_ready, {"pipe": above})

    @pl.when(pipe == 1)
    def _():
        pl.semaphore_wait(low_ready, 1)

    @pl.when(is_source)
    def _():
        signal(cross_ready, {"seq": sibling})
        for load in loads:
            load.wait()
        ld_copy().start()
        for h in range(heads):
            for i in range(4):
                y_copy(i, h).start()

    @pl.when(jnp.logical_and(is_source, core == 0))
    def _():
        for d in range(1, n_far + 1):

            @pl.when(d <= n_partner)
            def _():
                signal(ready.at[d - 1], {"seq": partner(d)})

    def make_aggregate(h):
        x_copy(h).wait_recv()
        agg_ref[h] = (
            jnp.exp(tot_ref[h : h + 1, :]) * sib_state_ref[h] + local_ref[1 - core, h]
        ).astype(BF16)

    @pl.when(is_source)
    def _():
        running_sums(ld_ref[0], part_ref, cum_ref, tot_ref)
        tot_copy().start()
        for h in range(heads):
            col = as_columns(cum_ref, h, half)
            lead = jnp.exp(col)
            tail_ref[h] = jnp.exp(tot_ref[h : h + 1, :] - col)
            query_weighted = (lead * cols(q_ref, h).astype(F32)).astype(BF16)
            local_ref[1, h] = mm_tn(query_weighted, cols(g_ref, h))

            @pl.when(core == 1)
            def _():
                x_copy(h).start()

        for h in range(heads):
            key_weighted = (tail_ref[h] * cols(k_ref, h).astype(F32)).astype(BF16)
            local_ref[0, h] = mm_tn(key_weighted, cols(v_ref, h))

            @pl.when(core == 0)
            def _():
                x_copy(h).start()

        tot_copy().wait_recv()
        chip_tot_ref[...] = tot_ref[...] + tot_sib_ref[...]

        @pl.when(core == 0)
        def _():
            for h in range(heads):
                make_aggregate(h)
            for i in range(n_far):

                @pl.when(i < n_partner)
                def _():
                    d = n_partner - i
                    tot_far(d).start()
                    for h in range(heads):
                        agg_far(d, h).start()

    at = lax.broadcasted_iota(jnp.int32, (half, half), 0)
    by = lax.broadcasted_iota(jnp.int32, (half, half), 1)
    lower, upper = at >= by, at <= by

    def inner_part(h):
        if h == 0:
            ld_copy().wait_recv()
            running_sums(up_ld_ref[0], part_ref, up_cum_ref, up_tot_ref)
        col = as_columns(up_cum_ref, h, half)
        up_lead_ref[h] = jnp.exp(col)
        up_tail_ref[h] = jnp.exp(up_tot_ref[h : h + 1, :] - col)
        for i in range(4):
            y_copy(i, h).wait_recv()
        q, g, k, v = (up_ref[i, h] for i in range(4))
        row0, row1 = up_cum_ref[h : h + 1, :half], up_cum_ref[h : h + 1, half:]
        col0, col1 = col[:half], col[half:]
        d00 = jnp.where(lower, jnp.exp(col0 - row0), 0.0)
        d10 = jnp.exp(col1 - row0)
        d11 = jnp.where(lower, jnp.exp(col1 - row1), 0.0)
        pair0 = (mm_nt(g[:half], v[:half]) * d00).astype(BF16)
        pair1 = (mm_nt(g[half:], v) * jnp.concatenate([d10, d11], axis=1)).astype(BF16)
        iq_ref[h, :half, :] = mm(pair0, k[:half])
        iq_ref[h, half:, :] = mm(pair1, k)
        e00 = jnp.where(upper, jnp.exp(row0 - col0), 0.0)
        e01 = jnp.exp(row1 - col0)
        e11 = jnp.where(upper, jnp.exp(row1 - col1), 0.0)
        e0 = jnp.concatenate([e00, e01], axis=1)
        pair_t0 = (mm_nt(v[:half], g) * e0).astype(BF16)
        pair_t1 = (mm_nt(v[half:], g[half:]) * e11).astype(BF16)
        ik_ref[h, :half, :] = mm(pair_t0, q)
        ik_ref[h, half:, :] = mm(pair_t1, q[half:])
        score_t0 = (mm_nt(k[:half], q) * e0).astype(BF16)
        score_t1 = (mm_nt(k[half:], q[half:]) * e11).astype(BF16)
        iv_ref[h, :half, :] = mm(score_t0, g)
        iv_ref[h, half:, :] = mm(score_t1, g[half:])

    def inner_parts(some):
        @pl.when(is_target)
        def _():
            for h in some:
                inner_part(h)

    inner_parts(range(heads // 2))

    @pl.when(jnp.logical_and(is_source, core == 1))
    def _():
        for h in range(heads):
            make_aggregate(h)
        for d in range(1, n_far + 1):

            @pl.when(d <= n_partner)
            def _():
                pl.semaphore_wait(ready.at[d - 1], 1)
                tot_far(d).start()
                for h in range(heads):
                    agg_far(d, h).start()

    inner_parts(range(heads // 2, heads - 1))

    @pl.when(is_source)
    def _():
        between = jnp.zeros(tot_ref.shape, F32)
        for d in range(1, n_far + 1):

            @pl.when(d <= n_partner)
            def _():
                tot_far(d).wait_recv()

            weight_ref[d - 1] = jnp.exp(between)
            between = between + far_tot_ref[d - 1]

        for h in range(heads):
            for d in range(1, n_far + 1):

                @pl.when(d <= n_partner)
                def _():
                    agg_far(d, h).wait_recv()

            total = jnp.zeros((size, size), F32)
            for d in range(1, n_far + 1):
                total = total + weight_ref[d - 1, h : h + 1, :] * far_ref[d - 1, h].astype(F32)
            ship_ref[0, h] = total.astype(BF16)
            ship_ref[1, h] = (
                jnp.exp(tot_ref[h : h + 1, :]) * total + local_ref[core, h]
            ).astype(BF16)
            if h == 0:
                pl.semaphore_wait(cross_ready, 1)
            st_copy(0, h).start()
            st_copy(1, h).start()

    inner_parts(range(heads - 1, heads))

    @pl.when(is_target)
    def _():
        for h in range(heads):
            here = slice(h * size, (h + 1) * size)
            g, k, v = (up_ref[i, h] for i in (1, 2, 3))
            for i in range(2):
                remote(
                    ship_ref.at[0, h],
                    up_state_ref.at[i, h],
                    st_send.at[0, h],
                    st_recv.at[i, h],
                    {"pipe": below},
                ).wait_recv()
            state_in, state_rev = up_state_ref[0, h], up_state_ref[1, h]
            lead, tail = up_lead_ref[h], up_tail_ref[h]
            oq_ref[0, :, here] = (iq_ref[h] + lead * mm_nt(g, state_in)).astype(BF16)
            ok_ref[0, :, here] = (ik_ref[h] + tail * mm_nt(v, state_rev)).astype(BF16)
            ov_ref[0, :, here] = (iv_ref[h] + tail * mm(k, state_rev)).astype(BF16)

    @pl.when(jnp.logical_not(is_target))
    def _():
        for o in (oq_ref, ok_ref, ov_ref):
            o[...] = jnp.zeros_like(o)

    @pl.when(is_source)
    def _():
        tot_copy().wait_send()
        for h in range(heads):
            x_copy(h).wait_send()
        for d in range(1, n_far + 1):

            @pl.when(d <= n_partner)
            def _():
                tot_far(d).wait_send()
                for h in range(heads):
                    agg_far(d, h).wait_send()

        ld_copy().wait_send()
        for h in range(heads):
            for i in range(4):
                y_copy(i, h).wait_send()
            for i in range(2):
                st_copy(i, h).wait_send()


def put_kernel(a_ref, b_ref, c_ref, oa_ref, ob_ref, oc_ref, sem):
    copies = [
        pltpu.make_async_copy(src, dst, sem.at[i])
        for i, (src, dst) in enumerate(((a_ref, oa_ref), (b_ref, ob_ref), (c_ref, oc_ref)))
    ]
    for copy in copies:
        copy.start()
    for copy in copies:
        copy.wait()


def per_device(n_pipe, n_seq, queries, keys, values, output_gradient, log_decay):
    length, width = queries.shape[1:]
    heads = log_decay.shape[1]
    size = width // heads
    n_chip = n_seq // 2
    n_far = n_chip - 1
    dma = pltpu.SemaphoreType.DMA
    tile = (8, size)
    anywhere = pl.BlockSpec(memory_space=pl.ANY)
    vmem = pl.BlockSpec(memory_space=pltpu.VMEM)
    shapes = [jax.ShapeDtypeStruct(queries.shape, BF16)] * 3
    results = pl.pallas_call(
        functools.partial(kernel, n_pipe, n_chip),
        out_shape=shapes,
        in_specs=[pl.BlockSpec(memory_space=pltpu.HBM)] * 5,
        out_specs=[vmem] * 3,
        scratch_shapes=[
            *[pltpu.VMEM((length, width), BF16)] * 4,
            pltpu.VMEM((1, heads, length), F32),
            pltpu.VMEM((16, length), F32),
            pltpu.VMEM((8, length), F32),
            *[pltpu.VMEM(tile, F32)] * 3,
            *[pltpu.VMEM((n_far, *tile), F32)] * 2,
            pltpu.VMEM((heads, length, size), F32),
            pltpu.VMEM((2, heads, size, size), F32),
            pltpu.VMEM((heads, size, size), F32),
            pltpu.VMEM((heads, size, size), BF16),
            pltpu.VMEM((n_far, heads, size, size), BF16),
            pltpu.VMEM((2, heads, size, size), BF16),
            pltpu.VMEM((4, heads, length, size), BF16),
            pltpu.VMEM((1, heads, length), F32),
            pltpu.VMEM((2, heads, size, size), BF16),
            pltpu.VMEM((8, length), F32),
            pltpu.VMEM(tile, F32),
            *[pltpu.VMEM((heads, length, size), F32)] * 5,
            dma((5,)),
            dma((1,)),
            dma((1,)),
            dma((heads,)),
            dma((heads,)),
            dma((n_far,)),
            dma((n_far,)),
            dma((n_far, heads)),
            dma((n_far, heads)),
            dma((1,)),
            dma((1,)),
            dma((4, heads)),
            dma((4, heads)),
            dma((2, heads)),
            dma((2, heads)),
            pltpu.SemaphoreType.REGULAR((n_far,)),
            pltpu.SemaphoreType.REGULAR,
            pltpu.SemaphoreType.REGULAR,
        ],
        compiler_params=pltpu.CompilerParams(
            collective_id=0, has_side_effects=True, vmem_limit_bytes=24 << 20
        ),
    )(
        *(
            pltpu.with_memory_space_constraint(x, pltpu.HBM)
            for x in (queries, keys, values, output_gradient, log_decay)
        )
    )
    return pl.pallas_call(
        put_kernel,
        out_shape=shapes,
        in_specs=[anywhere] * 3,
        out_specs=[anywhere] * 3,
        scratch_shapes=[dma((3,))],
        compiler_params=pltpu.CompilerParams(vmem_limit_bytes=4 << 20),
    )(*results)


def solution(mesh):
    in_specs = (
        P("pipe", "seq", "head"),
        P("pipe", "seq", "head"),
        P("pipe", "seq", "head"),
        P("pipe", "seq", "head"),
        P("pipe", "head", "seq"),
    )
    out_specs = (P("pipe", "seq", "head"), P("pipe", "seq", "head"), P("pipe", "seq", "head"))
    body = functools.partial(per_device, mesh.shape["pipe"], mesh.shape["seq"])
    return jax.shard_map(body, mesh=mesh, in_specs=in_specs, out_specs=out_specs, check_vma=False)
```

```python
import functools

import jax
import jax.numpy as jnp
from jax import lax
from jax.experimental import pallas as pl
from jax.experimental.pallas import tpu as pltpu
from jax.sharding import PartitionSpec as P

MESH = pl.DeviceIdType.MESH
INNER = (((1,), (1,)), ((), ()))
OUTER = (((0,), (0,)), ((), ()))
F32 = jnp.float32
BF16 = jnp.bfloat16


def mm(a, b):
    return jnp.dot(a, b, preferred_element_type=F32)


def mm_nt(a, b):
    return lax.dot_general(a, b, INNER, preferred_element_type=F32)


def mm_tn(a, b):
    return lax.dot_general(a, b, OUTER, preferred_element_type=F32)


def running_sums(ld, part_ref, cum_ref, tot_ref):
    heads, length = ld.shape
    high = ld.astype(BF16).astype(F32)
    rest = ld - high
    middle = rest.astype(BF16).astype(F32)
    part_ref[0:heads, :] = high
    part_ref[heads : 2 * heads, :] = middle
    part_ref[2 * heads : 3 * heads, :] = rest - middle
    earlier = (
        (
            lax.broadcasted_iota(jnp.int32, (length, length), 0)
            <= lax.broadcasted_iota(jnp.int32, (length, length), 1)
        )
        .astype(F32)
        .astype(BF16)
    )
    sums = mm(part_ref[...].astype(BF16), earlier)
    cum_ref[0:heads, :] = sums[0:heads] + sums[heads : 2 * heads] + sums[2 * heads : 3 * heads]
    tot_ref[...] = jnp.broadcast_to(cum_ref[:, length - 1 : length], tot_ref.shape)


def as_columns(cum_ref, h, half):
    blocks = []
    for b in range(2):
        row = cum_ref[h : h + 1, b * half : (b + 1) * half]
        blocks.append(jnp.broadcast_to(row, (half, half)).T)
    return jnp.concatenate(blocks, axis=0)


def kernel(
    n_pipe,
    n_chip,
    q_hbm,
    k_hbm,
    v_hbm,
    g_hbm,
    ld_hbm,
    oq_ref,
    ok_ref,
    ov_ref,
    q_ref,
    k_ref,
    v_ref,
    g_ref,
    ld_ref,
    part_ref,
    cum_ref,
    tot_ref,
    tot_sib_ref,
    chip_tot_ref,
    far_tot_ref,
    weight_ref,
    tail_ref,
    local_ref,
    sib_state_ref,
    agg_ref,
    far_ref,
    ship_ref,
    up_ref,
    up_ld_ref,
    up_state_ref,
    up_sib_state_ref,
    up_local_ref,
    up_sib_local_ref,
    up_cum_ref,
    up_tot_ref,
    up_tot_sib_ref,
    up_lead_ref,
    up_tail_ref,
    iq_ref,
    ik_ref,
    iv_ref,
    in_sem,
    tot_send,
    tot_recv,
    x_send,
    x_recv,
    ft_send,
    ft_recv,
    agg_send,
    agg_recv,
    ld_send,
    ld_recv,
    y_send,
    y_recv,
    st_send,
    st_recv,
    et_send,
    et_recv,
    ex_send,
    ex_recv,
    eu_send,
    eu_recv,
    ready,
    low_ready,
    cross_ready,
    sib_ready,
):
    length, width = q_ref.shape
    heads = ld_ref.shape[1]
    size = width // heads
    half = length // 2
    n_far = n_chip - 1

    pipe = lax.axis_index("pipe")
    seq = lax.axis_index("seq")
    chip = lax.div(seq, 2)
    core = lax.rem(seq, 2)
    sibling = seq + 1 - 2 * core
    step = 2 * core - 1
    n_partner = core * (n_far - chip) + (1 - core) * chip
    below = lax.rem(pipe + n_pipe - 1, n_pipe)
    above = lax.rem(pipe + 1, n_pipe)
    is_source = pipe > 0
    is_target = pipe < n_pipe - 1

    def partner(d):
        return 2 * (chip + step * d) + (1 - core)

    def cols(ref, h):
        return ref[:, h * size : (h + 1) * size]

    def remote(src, dst, send, recv, device):
        return pltpu.make_async_remote_copy(
            src_ref=src,
            dst_ref=dst,
            send_sem=send,
            recv_sem=recv,
            device_id=device,
            device_id_type=MESH,
        )

    def signal(sem, device):
        pl.semaphore_signal(sem, inc=1, device_id=device, device_id_type=MESH)

    inputs = (q_hbm, g_hbm, k_hbm, v_hbm)
    held = (q_ref, g_ref, k_ref, v_ref)

    def tot_copy():
        return remote(tot_ref, tot_sib_ref, tot_send.at[0], tot_recv.at[0], {"seq": sibling})

    def x_copy(h):
        return remote(
            local_ref.at[core, h], sib_state_ref.at[h], x_send.at[h], x_recv.at[h], {"seq": sibling}
        )

    def tot_far(d):
        return remote(
            chip_tot_ref,
            far_tot_ref.at[d - 1],
            ft_send.at[d - 1],
            ft_recv.at[d - 1],
            {"seq": partner(d)},
        )

    def agg_far(d, h):
        return remote(
            agg_ref.at[h],
            far_ref.at[d - 1, h],
            agg_send.at[d - 1, h],
            agg_recv.at[d - 1, h],
            {"seq": partner(d)},
        )

    def ld_copy():
        return remote(ld_ref, up_ld_ref, ld_send.at[0], ld_recv.at[0], {"pipe": below})

    def y_copy(i, h):
        return remote(
            held[i].at[:, pl.ds(h * size, size)],
            up_ref.at[i, h],
            y_send.at[i, h],
            y_recv.at[i, h],
            {"pipe": below},
        )

    def st_copy(h):
        return remote(
            ship_ref.at[h],
            up_state_ref.at[core, h],
            st_send.at[h],
            st_recv.at[h],
            {"pipe": below},
        )

    def up_tot_copy():
        return remote(up_tot_ref, up_tot_sib_ref, et_send.at[0], et_recv.at[0], {"seq": sibling})

    def up_local_copy(h):
        return remote(
            up_local_ref.at[h], up_sib_local_ref.at[h], ex_send.at[h], ex_recv.at[h], {"seq": sibling}
        )

    def up_state_copy(h):
        return remote(
            up_state_ref.at[core, h],
            up_sib_state_ref.at[h],
            eu_send.at[h],
            eu_recv.at[h],
            {"seq": sibling},
        )

    barrier = pltpu.get_barrier_semaphore()
    busy = jnp.minimum(pipe, 1)

    @pl.when(is_source)
    def _():
        signal(barrier, {"seq": sibling})

    @pl.when(pipe == 1)
    def _():
        signal(barrier, {"pipe": below})

    @pl.when(jnp.logical_and(is_source, is_target))
    def _():
        signal(barrier, {"pipe": above})

    loads = [pltpu.make_async_copy(ld_hbm, ld_ref, in_sem.at[4])]
    for i, (src, dst) in enumerate(zip(inputs, held)):
        loads.append(pltpu.make_async_copy(src.at[0], dst, in_sem.at[i]))
    @pl.when(is_source)
    def _():
        for load in loads:
            load.start()

    pl.semaphore_wait(barrier, 1 + busy * jnp.minimum(chip, 1) + jnp.minimum(lax.div(pipe, 2), 1))

    @pl.when(jnp.logical_and(is_source, chip < n_far))
    def _():
        signal(barrier, {"seq": seq + 2})

    @pl.when(pipe == 0)
    def _():
        signal(low_ready, {"pipe": above})

    @pl.when(pipe == 1)
    def _():
        pl.semaphore_wait(low_ready, 1)
        signal(cross_ready, {"seq": sibling})

    @pl.when(is_source)
    def _():
        for load in loads:
            load.wait()
        ld_copy().start()
        for h in range(heads):
            for i in range(4):
                y_copy(i, h).start()

    @pl.when(jnp.logical_and(is_source, core == 0))
    def _():
        for d in range(1, n_far + 1):

            @pl.when(d <= n_partner)
            def _():
                signal(ready.at[d - 1], {"seq": partner(d)})

    for d in range(1, n_far + 1):

        @pl.when(d > n_partner)
        def _():
            far_ref[d - 1] = jnp.zeros(far_ref.shape[1:], BF16)
            far_tot_ref[d - 1] = jnp.zeros(far_tot_ref.shape[1:], F32)

    part_ref[...] = jnp.zeros_like(part_ref)
    cum_ref[...] = jnp.zeros_like(cum_ref)
    up_cum_ref[...] = jnp.zeros_like(up_cum_ref)

    def make_aggregate(h):
        x_copy(h).wait_recv()
        agg_ref[h] = (
            jnp.exp(tot_ref[h : h + 1, :]) * sib_state_ref[h] + local_ref[1 - core, h]
        ).astype(BF16)

    @pl.when(is_source)
    def _():
        running_sums(ld_ref[0], part_ref, cum_ref, tot_ref)
        tot_copy().start()
        for h in range(heads):
            col = as_columns(cum_ref, h, half)
            lead = jnp.exp(col)
            tail_ref[h] = jnp.exp(tot_ref[h : h + 1, :] - col)
            query_weighted = (lead * cols(q_ref, h).astype(F32)).astype(BF16)
            local_ref[1, h] = mm_tn(query_weighted, cols(g_ref, h))

            @pl.when(core == 1)
            def _():
                x_copy(h).start()

        for h in range(heads):
            key_weighted = (tail_ref[h] * cols(k_ref, h).astype(F32)).astype(BF16)
            local_ref[0, h] = mm_tn(key_weighted, cols(v_ref, h))

            @pl.when(core == 0)
            def _():
                x_copy(h).start()

        tot_copy().wait_recv()
        chip_tot_ref[...] = tot_ref[...] + tot_sib_ref[...]

        @pl.when(core == 0)
        def _():
            for h in range(heads):
                make_aggregate(h)
            for i in range(n_far):

                @pl.when(i < n_partner)
                def _():
                    d = n_partner - i
                    tot_far(d).start()
                    for h in range(heads):
                        agg_far(d, h).start()

    at = lax.broadcasted_iota(jnp.int32, (half, half), 0)
    by = lax.broadcasted_iota(jnp.int32, (half, half), 1)
    lower, upper = at >= by, at <= by

    def inner_part(h):
        if h == 0:
            ld_copy().wait_recv()
            running_sums(up_ld_ref[0], part_ref, up_cum_ref, up_tot_ref)
        col = as_columns(up_cum_ref, h, half)
        up_lead_ref[h] = jnp.exp(col)
        up_tail_ref[h] = jnp.exp(up_tot_ref[h : h + 1, :] - col)
        for i in range(4):
            y_copy(i, h).wait_recv()
        q, g, k, v = (up_ref[i, h] for i in range(4))
        row0, row1 = up_cum_ref[h : h + 1, :half], up_cum_ref[h : h + 1, half:]
        col0, col1 = col[:half], col[half:]
        d00 = jnp.where(lower, jnp.exp(col0 - row0), 0.0)
        d10 = jnp.exp(col1 - row0)
        d11 = jnp.where(lower, jnp.exp(col1 - row1), 0.0)
        pair0 = (mm_nt(g[:half], v[:half]) * d00).astype(BF16)
        pair1 = (mm_nt(g[half:], v) * jnp.concatenate([d10, d11], axis=1)).astype(BF16)
        iq_ref[h, :half, :] = mm(pair0, k[:half])
        iq_ref[h, half:, :] = mm(pair1, k)
        e00 = jnp.where(upper, jnp.exp(row0 - col0), 0.0)
        e01 = jnp.exp(row1 - col0)
        e11 = jnp.where(upper, jnp.exp(row1 - col1), 0.0)
        e0 = jnp.concatenate([e00, e01], axis=1)
        pair_t0 = (mm_nt(v[:half], g) * e0).astype(BF16)
        pair_t1 = (mm_nt(v[half:], g[half:]) * e11).astype(BF16)
        ik_ref[h, :half, :] = mm(pair_t0, q)
        ik_ref[h, half:, :] = mm(pair_t1, q[half:])
        score_t0 = (mm_nt(k[:half], q) * e0).astype(BF16)
        score_t1 = (mm_nt(k[half:], q[half:]) * e11).astype(BF16)
        iv_ref[h, :half, :] = mm(score_t0, g)
        iv_ref[h, half:, :] = mm(score_t1, g[half:])

        @pl.when(core == 0)
        def _():
            key_weighted = (up_tail_ref[h] * k.astype(F32)).astype(BF16)
            up_local_ref[h] = mm_tn(key_weighted, v)

        @pl.when(core == 1)
        def _():
            query_weighted = (up_lead_ref[h] * q.astype(F32)).astype(BF16)
            up_local_ref[h] = mm_tn(query_weighted, g)

    def inner_parts(some):
        @pl.when(is_target)
        def _():
            for h in some:
                inner_part(h)

    def exchange(some):
        @pl.when(is_target)
        def _():
            for h in some:
                if h == 0:
                    up_tot_copy().start()
                up_local_copy(h).start()

    inner_parts(range(heads // 2))

    @pl.when(pipe == 1)
    def _():
        pl.semaphore_wait(cross_ready, 1)
        signal(sib_ready, {"pipe": below})

    @pl.when(jnp.logical_and(is_source, core == 1))
    def _():
        for h in range(heads):
            make_aggregate(h)
        for d in range(1, n_far + 1):

            @pl.when(d <= n_partner)
            def _():
                pl.semaphore_wait(ready.at[d - 1], 1)
                tot_far(d).start()
                for h in range(heads):
                    agg_far(d, h).start()

    inner_parts(range(heads // 2, heads - 1))

    @pl.when(pipe == 0)
    def _():
        pl.semaphore_wait(sib_ready, 1)

    exchange(range(heads - 1))

    @pl.when(is_source)
    def _():
        between = jnp.zeros(tot_ref.shape, F32)
        for d in range(1, n_far + 1):

            @pl.when(d <= n_partner)
            def _():
                tot_far(d).wait_recv()

            weight_ref[d - 1] = jnp.exp(between)
            between = between + far_tot_ref[d - 1]

        for h in range(heads):
            for d in range(1, n_far + 1):

                @pl.when(d <= n_partner)
                def _():
                    agg_far(d, h).wait_recv()

            total = jnp.zeros((size, size), F32)
            for d in range(1, n_far + 1):
                total = total + weight_ref[d - 1, h : h + 1, :] * far_ref[d - 1, h].astype(F32)
            ship_ref[h] = total.astype(BF16)
            st_copy(h).start()

    inner_parts(range(heads - 1, heads))
    exchange(range(heads - 1, heads))

    @pl.when(is_target)
    def _():
        for h in range(heads):
            st_copy(h).wait_recv()
            up_state_copy(h).start()
        up_tot_copy().wait_recv()
        for h in range(heads):
            here = slice(h * size, (h + 1) * size)
            g, k, v = (up_ref[i, h] for i in (1, 2, 3))
            up_local_copy(h).wait_recv()
            up_state_copy(h).wait_recv()
            up_state_ref[1 - core, h] = (
                jnp.exp(up_tot_sib_ref[h : h + 1, :]) * up_sib_state_ref[h].astype(F32)
                + up_sib_local_ref[h]
            ).astype(BF16)
            state_in, state_rev = up_state_ref[0, h], up_state_ref[1, h]
            lead, tail = up_lead_ref[h], up_tail_ref[h]
            oq_ref[0, :, here] = (iq_ref[h] + lead * mm_nt(g, state_in)).astype(BF16)
            ok_ref[0, :, here] = (ik_ref[h] + tail * mm_nt(v, state_rev)).astype(BF16)
            ov_ref[0, :, here] = (iv_ref[h] + tail * mm(k, state_rev)).astype(BF16)

    @pl.when(jnp.logical_not(is_target))
    def _():
        for o in (oq_ref, ok_ref, ov_ref):
            o[...] = jnp.zeros_like(o)

    @pl.when(is_source)
    def _():
        tot_copy().wait_send()
        for h in range(heads):
            x_copy(h).wait_send()
        for d in range(1, n_far + 1):

            @pl.when(d <= n_partner)
            def _():
                tot_far(d).wait_send()
                for h in range(heads):
                    agg_far(d, h).wait_send()

        ld_copy().wait_send()
        for h in range(heads):
            for i in range(4):
                y_copy(i, h).wait_send()
            st_copy(h).wait_send()

    @pl.when(is_target)
    def _():
        up_tot_copy().wait_send()
        for h in range(heads):
            up_local_copy(h).wait_send()
            up_state_copy(h).wait_send()


def put_kernel(a_ref, b_ref, c_ref, oa_ref, ob_ref, oc_ref, sem):
    copies = [
        pltpu.make_async_copy(src, dst, sem.at[i])
        for i, (src, dst) in enumerate(((a_ref, oa_ref), (b_ref, ob_ref), (c_ref, oc_ref)))
    ]
    for copy in copies:
        copy.start()
    for copy in copies:
        copy.wait()


def per_device(n_pipe, n_seq, queries, keys, values, output_gradient, log_decay):
    length, width = queries.shape[1:]
    heads = log_decay.shape[1]
    size = width // heads
    n_chip = n_seq // 2
    n_far = n_chip - 1
    dma = pltpu.SemaphoreType.DMA
    tile = (8, size)
    anywhere = pl.BlockSpec(memory_space=pl.ANY)
    vmem = pl.BlockSpec(memory_space=pltpu.VMEM)
    shapes = [jax.ShapeDtypeStruct(queries.shape, BF16)] * 3
    results = pl.pallas_call(
        functools.partial(kernel, n_pipe, n_chip),
        out_shape=shapes,
        in_specs=[pl.BlockSpec(memory_space=pltpu.HBM)] * 5,
        out_specs=[vmem] * 3,
        scratch_shapes=[
            *[pltpu.VMEM((length, width), BF16)] * 4,
            pltpu.VMEM((1, heads, length), F32),
            pltpu.VMEM((16, length), F32),
            pltpu.VMEM((8, length), F32),
            *[pltpu.VMEM(tile, F32)] * 3,
            *[pltpu.VMEM((n_far, *tile), F32)] * 2,
            pltpu.VMEM((heads, length, size), F32),
            pltpu.VMEM((2, heads, size, size), F32),
            pltpu.VMEM((heads, size, size), F32),
            pltpu.VMEM((heads, size, size), BF16),
            pltpu.VMEM((n_far, heads, size, size), BF16),
            pltpu.VMEM((heads, size, size), BF16),
            pltpu.VMEM((4, heads, length, size), BF16),
            pltpu.VMEM((1, heads, length), F32),
            pltpu.VMEM((2, heads, size, size), BF16),
            pltpu.VMEM((heads, size, size), BF16),
            *[pltpu.VMEM((heads, size, size), F32)] * 2,
            pltpu.VMEM((8, length), F32),
            *[pltpu.VMEM(tile, F32)] * 2,
            *[pltpu.VMEM((heads, length, size), F32)] * 5,
            dma((5,)),
            dma((1,)),
            dma((1,)),
            dma((heads,)),
            dma((heads,)),
            dma((n_far,)),
            dma((n_far,)),
            dma((n_far, heads)),
            dma((n_far, heads)),
            dma((1,)),
            dma((1,)),
            dma((4, heads)),
            dma((4, heads)),
            dma((heads,)),
            dma((heads,)),
            dma((1,)),
            dma((1,)),
            *[dma((heads,))] * 4,
            pltpu.SemaphoreType.REGULAR((n_far,)),
            *[pltpu.SemaphoreType.REGULAR] * 3,
        ],
        compiler_params=pltpu.CompilerParams(
            collective_id=0, has_side_effects=True, vmem_limit_bytes=24 << 20
        ),
    )(
        *(
            pltpu.with_memory_space_constraint(x, pltpu.HBM)
            for x in (queries, keys, values, output_gradient, log_decay)
        )
    )
    return pl.pallas_call(
        put_kernel,
        out_shape=shapes,
        in_specs=[anywhere] * 3,
        out_specs=[anywhere] * 3,
        scratch_shapes=[dma((3,))],
        compiler_params=pltpu.CompilerParams(vmem_limit_bytes=4 << 20),
    )(*results)


def solution(mesh):
    in_specs = (
        P("pipe", "seq", "head"),
        P("pipe", "seq", "head"),
        P("pipe", "seq", "head"),
        P("pipe", "seq", "head"),
        P("pipe", "head", "seq"),
    )
    out_specs = (P("pipe", "seq", "head"), P("pipe", "seq", "head"), P("pipe", "seq", "head"))
    body = functools.partial(per_device, mesh.shape["pipe"], mesh.shape["seq"])
    return jax.shard_map(body, mesh=mesh, in_specs=in_specs, out_specs=out_specs, check_vma=False)
```

```python
import functools

import jax
import jax.numpy as jnp
from jax import lax
from jax.experimental import pallas as pl
from jax.experimental.pallas import tpu as pltpu
from jax.sharding import PartitionSpec as P

MESH = pl.DeviceIdType.MESH
INNER = (((1,), (1,)), ((), ()))
OUTER = (((0,), (0,)), ((), ()))
F32 = jnp.float32
BF16 = jnp.bfloat16


def mm(a, b):
    return jnp.dot(a, b, preferred_element_type=F32)


def mm_nt(a, b):
    return lax.dot_general(a, b, INNER, preferred_element_type=F32)


def mm_tn(a, b):
    return lax.dot_general(a, b, OUTER, preferred_element_type=F32)


def running_sums(ld, part_ref, cum_ref, tot_ref):
    heads, length = ld.shape
    high = ld.astype(BF16).astype(F32)
    rest = ld - high
    middle = rest.astype(BF16).astype(F32)
    part_ref[0:heads, :] = high
    part_ref[heads : 2 * heads, :] = middle
    part_ref[2 * heads : 3 * heads, :] = rest - middle
    earlier = (
        (
            lax.broadcasted_iota(jnp.int32, (length, length), 0)
            <= lax.broadcasted_iota(jnp.int32, (length, length), 1)
        )
        .astype(F32)
        .astype(BF16)
    )
    sums = mm(part_ref[...].astype(BF16), earlier)
    cum_ref[0:heads, :] = sums[0:heads] + sums[heads : 2 * heads] + sums[2 * heads : 3 * heads]
    tot_ref[...] = jnp.broadcast_to(cum_ref[:, length - 1 : length], tot_ref.shape)


def as_columns(cum_ref, h, half):
    blocks = []
    for b in range(2):
        row = cum_ref[h : h + 1, b * half : (b + 1) * half]
        blocks.append(jnp.broadcast_to(row, (half, half)).T)
    return jnp.concatenate(blocks, axis=0)


def weighted_state(x, weights, y):
    return mm((x.T.astype(F32) * weights).astype(BF16), y)


def kernel(
    n_pipe,
    n_chip,
    n_late,
    q_hbm,
    k_hbm,
    v_hbm,
    g_hbm,
    ld_hbm,
    oq_ref,
    ok_ref,
    ov_ref,
    q_ref,
    k_ref,
    v_ref,
    g_ref,
    ld_ref,
    part_ref,
    cum_ref,
    tot_ref,
    tot_sib_ref,
    chip_tot_ref,
    far_tot_ref,
    weight_ref,
    local_ref,
    sib_state_ref,
    agg_ref,
    far_ref,
    ship_ref,
    up_ref,
    up_ld_ref,
    up_state_ref,
    up_sib_state_ref,
    up_local_ref,
    up_sib_local_ref,
    up_cum_ref,
    up_tot_ref,
    up_tot_sib_ref,
    up_lead_ref,
    up_tail_ref,
    iq_ref,
    ik_ref,
    iv_ref,
    in_sem,
    tot_send,
    tot_recv,
    x_send,
    x_recv,
    ft_send,
    ft_recv,
    agg_send,
    agg_recv,
    ld_send,
    ld_recv,
    y_send,
    y_recv,
    st_send,
    st_recv,
    et_send,
    et_recv,
    ex_send,
    ex_recv,
    eu_send,
    eu_recv,
    ready,
    low_ready,
    cross_ready,
    sib_ready,
):
    length, width = q_ref.shape
    heads = ld_ref.shape[1]
    size = width // heads
    half = length // 2
    n_far = n_chip - 1

    pipe = lax.axis_index("pipe")
    seq = lax.axis_index("seq")
    chip = lax.div(seq, 2)
    core = lax.rem(seq, 2)
    sibling = seq + 1 - 2 * core
    step = 2 * core - 1
    n_partner = core * (n_far - chip) + (1 - core) * chip
    below = lax.rem(pipe + n_pipe - 1, n_pipe)
    above = lax.rem(pipe + 1, n_pipe)
    is_source = pipe > 0
    is_target = pipe < n_pipe - 1
    late_states = chip < n_late

    def partner(d):
        return 2 * (chip + step * d) + (1 - core)

    def cols(ref, h):
        return ref[:, h * size : (h + 1) * size]

    def remote(src, dst, send, recv, device):
        return pltpu.make_async_remote_copy(
            src_ref=src,
            dst_ref=dst,
            send_sem=send,
            recv_sem=recv,
            device_id=device,
            device_id_type=MESH,
        )

    def signal(sem, device):
        pl.semaphore_signal(sem, inc=1, device_id=device, device_id_type=MESH)

    inputs = (q_hbm, g_hbm, k_hbm, v_hbm)
    held = (q_ref, g_ref, k_ref, v_ref)

    def tot_copy():
        return remote(tot_ref, tot_sib_ref, tot_send.at[0], tot_recv.at[0], {"seq": sibling})

    def x_copy():
        return remote(
            local_ref.at[core], sib_state_ref, x_send.at[0], x_recv.at[0], {"seq": sibling}
        )

    def tot_far(d):
        return remote(
            chip_tot_ref,
            far_tot_ref.at[d - 1],
            ft_send.at[d - 1],
            ft_recv.at[d - 1],
            {"seq": partner(d)},
        )

    def agg_far(d):
        return remote(
            agg_ref,
            far_ref.at[d - 1],
            agg_send.at[d - 1],
            agg_recv.at[d - 1],
            {"seq": partner(d)},
        )

    def ld_copy():
        return remote(ld_ref, up_ld_ref, ld_send.at[0], ld_recv.at[0], {"pipe": below})

    def y_copy(i, h):
        return remote(
            held[i].at[:, pl.ds(h * size, size)],
            up_ref.at[i, h],
            y_send.at[i, h],
            y_recv.at[i, h],
            {"pipe": below},
        )

    def st_copy(h):
        return remote(
            ship_ref.at[h],
            up_state_ref.at[core, h],
            st_send.at[h],
            st_recv.at[h],
            {"pipe": below},
        )

    def up_tot_copy():
        return remote(up_tot_ref, up_tot_sib_ref, et_send.at[0], et_recv.at[0], {"seq": sibling})

    def up_local_copy(h):
        return remote(
            up_local_ref.at[h], up_sib_local_ref.at[h], ex_send.at[h], ex_recv.at[h], {"seq": sibling}
        )

    def up_state_copy(h):
        return remote(
            up_state_ref.at[core, h],
            up_sib_state_ref.at[h],
            eu_send.at[h],
            eu_recv.at[h],
            {"seq": sibling},
        )

    def ship(some):
        for which, order in ((0, (2, 3, 0, 1)), (1, (0, 1, 2, 3))):

            @pl.when(core == which)
            def _():
                for h in some:
                    for i in order:
                        y_copy(i, h).start()

    barrier = pltpu.get_barrier_semaphore()
    busy = jnp.minimum(pipe, 1)

    @pl.when(is_source)
    def _():
        signal(barrier, {"seq": sibling})

    @pl.when(pipe == 1)
    def _():
        signal(barrier, {"pipe": below})

    @pl.when(jnp.logical_and(is_source, is_target))
    def _():
        signal(barrier, {"pipe": above})

    loads = [pltpu.make_async_copy(ld_hbm, ld_ref, in_sem.at[4])]
    for i, (src, dst) in enumerate(zip(inputs, held)):
        loads.append(pltpu.make_async_copy(src.at[0], dst, in_sem.at[i]))
    @pl.when(is_source)
    def _():
        for load in loads:
            load.start()

    pl.semaphore_wait(barrier, 1 + busy * jnp.minimum(chip, 1) + jnp.minimum(lax.div(pipe, 2), 1))

    @pl.when(jnp.logical_and(is_source, chip < n_far))
    def _():
        signal(barrier, {"seq": seq + 2})

    @pl.when(pipe == 0)
    def _():
        signal(low_ready, {"pipe": above})

    @pl.when(pipe == 1)
    def _():
        pl.semaphore_wait(low_ready, 1)
        signal(cross_ready, {"seq": sibling})

    @pl.when(is_source)
    def _():
        for load in loads:
            load.wait()
        ld_copy().start()
        ship(range(heads - 1))

    last_first = jnp.logical_and(late_states, core == 1)

    @pl.when(jnp.logical_and(is_source, last_first))
    def _():
        ship(range(heads - 1, heads))

    @pl.when(jnp.logical_and(is_source, core == 0))
    def _():
        for d in range(1, n_far + 1):

            @pl.when(d <= n_partner)
            def _():
                signal(ready.at[d - 1], {"seq": partner(d)})

    part_ref[...] = jnp.zeros_like(part_ref)
    cum_ref[...] = jnp.zeros_like(cum_ref)
    up_cum_ref[...] = jnp.zeros_like(up_cum_ref)

    def make_aggregates():
        x_copy().wait_recv()
        for h in range(heads):
            agg_ref[h] = (
                jnp.exp(tot_ref[h : h + 1, :]) * sib_state_ref[h] + local_ref[1 - core, h]
            ).astype(BF16)

    @pl.when(is_source)
    def _():
        running_sums(ld_ref[0], part_ref, cum_ref, tot_ref)
        tot_copy().start()
        lead = jnp.exp(cum_ref[...])
        tail = jnp.exp(tot_ref[:, :1] - cum_ref[...])
        for h in range(heads):
            local_ref[1, h] = weighted_state(cols(q_ref, h), lead[h : h + 1, :], cols(g_ref, h))

        @pl.when(core == 1)
        def _():
            x_copy().start()

        for h in range(heads):
            local_ref[0, h] = weighted_state(cols(k_ref, h), tail[h : h + 1, :], cols(v_ref, h))

        @pl.when(core == 0)
        def _():
            x_copy().start()

        tot_copy().wait_recv()
        chip_tot_ref[...] = tot_ref[...] + tot_sib_ref[...]

        @pl.when(core == 0)
        def _():
            make_aggregates()
            for i in range(n_far):

                @pl.when(i < n_partner)
                def _():
                    d = n_partner - i
                    tot_far(d).start()
                    agg_far(d).start()

    for d in range(1, n_far + 1):

        @pl.when(d > n_partner)
        def _():
            far_ref[d - 1] = jnp.zeros(far_ref.shape[1:], BF16)
            far_tot_ref[d - 1] = jnp.zeros(far_tot_ref.shape[1:], F32)

    at = lax.broadcasted_iota(jnp.int32, (half, half), 0)
    by = lax.broadcasted_iota(jnp.int32, (half, half), 1)
    lower, upper = at >= by, at <= by

    def sibling_part(h):
        if h == 0:
            ld_copy().wait_recv()
            running_sums(up_ld_ref[0], part_ref, up_cum_ref, up_tot_ref)
        row = up_cum_ref[h : h + 1, :]

        @pl.when(core == 0)
        def _():
            y_copy(2, h).wait_recv()
            y_copy(3, h).wait_recv()
            weights = jnp.exp(up_tot_ref[h : h + 1, :1] - row)
            up_local_ref[h] = weighted_state(up_ref[2, h], weights, up_ref[3, h])

        @pl.when(core == 1)
        def _():
            y_copy(0, h).wait_recv()
            y_copy(1, h).wait_recv()
            up_local_ref[h] = weighted_state(up_ref[0, h], jnp.exp(row), up_ref[1, h])

    def inner_part(h):
        col = as_columns(up_cum_ref, h, half)
        up_lead_ref[h] = jnp.exp(col)
        up_tail_ref[h] = jnp.exp(up_tot_ref[h : h + 1, :] - col)
        for which, rest in ((0, (0, 1)), (1, (2, 3))):

            @pl.when(core == which)
            def _():
                for i in rest:
                    y_copy(i, h).wait_recv()

        q, g, k, v = (up_ref[i, h] for i in range(4))
        row0, row1 = up_cum_ref[h : h + 1, :half], up_cum_ref[h : h + 1, half:]
        col0, col1 = col[:half], col[half:]
        d00 = jnp.where(lower, jnp.exp(col0 - row0), 0.0)
        d10 = jnp.exp(col1 - row0)
        d11 = jnp.where(lower, jnp.exp(col1 - row1), 0.0)
        pair0 = (mm_nt(g[:half], v[:half]) * d00).astype(BF16)
        pair1 = (mm_nt(g[half:], v) * jnp.concatenate([d10, d11], axis=1)).astype(BF16)
        iq_ref[h, :half, :] = mm(pair0, k[:half])
        iq_ref[h, half:, :] = mm(pair1, k)
        e00 = jnp.where(upper, jnp.exp(row0 - col0), 0.0)
        e01 = jnp.exp(row1 - col0)
        e11 = jnp.where(upper, jnp.exp(row1 - col1), 0.0)
        e0 = jnp.concatenate([e00, e01], axis=1)
        pair_t0 = (mm_nt(v[:half], g) * e0).astype(BF16)
        pair_t1 = (mm_nt(v[half:], g[half:]) * e11).astype(BF16)
        ik_ref[h, :half, :] = mm(pair_t0, q)
        ik_ref[h, half:, :] = mm(pair_t1, q[half:])
        score_t0 = (mm_nt(k[:half], q) * e0).astype(BF16)
        score_t1 = (mm_nt(k[half:], q[half:]) * e11).astype(BF16)
        iv_ref[h, :half, :] = mm(score_t0, g)
        iv_ref[h, half:, :] = mm(score_t1, g[half:])

    def result(h):
        here = slice(h * size, (h + 1) * size)
        g, k, v = (up_ref[i, h] for i in (1, 2, 3))
        up_local_copy(h).wait_recv()
        up_state_copy(h).wait_recv()
        up_state_ref[1 - core, h] = (
            jnp.exp(up_tot_sib_ref[h : h + 1, :]) * up_sib_state_ref[h].astype(F32)
            + up_sib_local_ref[h]
        ).astype(BF16)
        state_in, state_rev = up_state_ref[0, h], up_state_ref[1, h]
        for b in range(2):
            rows = slice(b * half, (b + 1) * half)
            lead, tail = up_lead_ref[h, rows, :], up_tail_ref[h, rows, :]
            oq_ref[0, rows, here] = (
                iq_ref[h, rows, :] + lead * mm_nt(g[rows], state_in)
            ).astype(BF16)
            ok_ref[0, rows, here] = (
                ik_ref[h, rows, :] + tail * mm_nt(v[rows], state_rev)
            ).astype(BF16)
            ov_ref[0, rows, here] = (iv_ref[h, rows, :] + tail * mm(k[rows], state_rev)).astype(
                BF16
            )

    half_heads = heads // 2

    @pl.when(jnp.logical_and(is_source, core == 1))
    def _():
        make_aggregates()
        for d in range(1, n_far + 1):

            @pl.when(d <= n_partner)
            def _():
                pl.semaphore_wait(ready.at[d - 1], 1)
                tot_far(d).start()
                agg_far(d).start()

    @pl.when(is_target)
    def _():
        for h in range(half_heads):
            sibling_part(h)
            inner_part(h)

    @pl.when(pipe == 1)
    def _():
        pl.semaphore_wait(cross_ready, 1)
        signal(sib_ready, {"pipe": below})

    def middle_heads():
        up_tot_copy().start()
        for h in range(half_heads):
            up_local_copy(h).start()
        for h in range(half_heads, heads - 1):
            sibling_part(h)
            up_local_copy(h).start()
            inner_part(h)

    @pl.when(pipe == 0)
    def _():
        pl.semaphore_wait(sib_ready, 1)

    @pl.when(jnp.logical_and(is_target, last_first))
    def _():
        middle_heads()

    @pl.when(is_source)
    def _():
        between = jnp.zeros(tot_ref.shape, F32)
        for d in range(1, n_far + 1):

            @pl.when(d <= n_partner)
            def _():
                tot_far(d).wait_recv()
                agg_far(d).wait_recv()

            weight_ref[d - 1] = jnp.exp(between)
            between = between + far_tot_ref[d - 1]

        for h in range(heads):
            total = jnp.zeros((size, size), F32)
            for d in range(1, n_far + 1):
                total = total + weight_ref[d - 1, h : h + 1, :] * far_ref[d - 1, h].astype(F32)
            ship_ref[h] = total.astype(BF16)
            st_copy(h).start()

    @pl.when(jnp.logical_and(is_source, jnp.logical_not(last_first)))
    def _():
        ship(range(heads - 1, heads))

    @pl.when(jnp.logical_and(is_target, jnp.logical_not(last_first)))
    def _():
        middle_heads()

    @pl.when(jnp.logical_and(is_target, last_first))
    def _():
        sibling_part(heads - 1)
        up_local_copy(heads - 1).start()
        inner_part(heads - 1)

    @pl.when(is_target)
    def _():
        for h in range(heads):
            st_copy(h).wait_recv()
            up_state_copy(h).start()
        up_tot_copy().wait_recv()

    @pl.when(jnp.logical_and(is_target, jnp.logical_not(last_first)))
    def _():
        sibling_part(heads - 1)
        up_local_copy(heads - 1).start()

    @pl.when(jnp.logical_and(is_target, jnp.logical_not(late_states)))
    def _():
        for h in range(heads - 1):
            result(h)

    @pl.when(jnp.logical_and(is_target, jnp.logical_not(last_first)))
    def _():
        inner_part(heads - 1)

    @pl.when(is_source)
    def _():
        tot_copy().wait_send()
        x_copy().wait_send()
        for d in range(1, n_far + 1):

            @pl.when(d <= n_partner)
            def _():
                tot_far(d).wait_send()
                agg_far(d).wait_send()

        ld_copy().wait_send()
        for h in range(heads):
            for i in range(4):
                y_copy(i, h).wait_send()
            st_copy(h).wait_send()

    @pl.when(jnp.logical_and(is_target, late_states))
    def _():
        for h in range(heads - 1):
            result(h)

    @pl.when(is_target)
    def _():
        result(heads - 1)
        up_tot_copy().wait_send()
        for h in range(heads):
            up_local_copy(h).wait_send()

    @pl.when(jnp.logical_not(is_target))
    def _():
        for o in (oq_ref, ok_ref, ov_ref):
            o[...] = jnp.zeros_like(o)

    @pl.when(is_target)
    def _():
        for h in range(heads):
            up_state_copy(h).wait_send()


def put_kernel(a_ref, b_ref, c_ref, oa_ref, ob_ref, oc_ref, sem):
    copies = [
        pltpu.make_async_copy(src, dst, sem.at[i])
        for i, (src, dst) in enumerate(((a_ref, oa_ref), (b_ref, ob_ref), (c_ref, oc_ref)))
    ]
    for copy in copies:
        copy.start()
    for copy in copies:
        copy.wait()


def per_device(n_pipe, n_seq, queries, keys, values, output_gradient, log_decay):
    length, width = queries.shape[1:]
    heads = log_decay.shape[1]
    size = width // heads
    n_chip = n_seq // 2
    n_far = n_chip - 1
    dma = pltpu.SemaphoreType.DMA
    tile = (8, size)
    anywhere = pl.BlockSpec(memory_space=pl.ANY)
    vmem = pl.BlockSpec(memory_space=pltpu.VMEM)
    shapes = [jax.ShapeDtypeStruct(queries.shape, BF16)] * 3
    results = pl.pallas_call(
        functools.partial(kernel, n_pipe, n_chip, n_chip // 2),
        out_shape=shapes,
        in_specs=[pl.BlockSpec(memory_space=pltpu.HBM)] * 5,
        out_specs=[vmem] * 3,
        scratch_shapes=[
            *[pltpu.VMEM((length, width), BF16)] * 4,
            pltpu.VMEM((1, heads, length), F32),
            pltpu.VMEM((16, length), F32),
            pltpu.VMEM((8, length), F32),
            *[pltpu.VMEM(tile, F32)] * 3,
            *[pltpu.VMEM((n_far, *tile), F32)] * 2,
            pltpu.VMEM((2, heads, size, size), F32),
            pltpu.VMEM((heads, size, size), F32),
            pltpu.VMEM((heads, size, size), BF16),
            pltpu.VMEM((n_far, heads, size, size), BF16),
            pltpu.VMEM((heads, size, size), BF16),
            pltpu.VMEM((4, heads, length, size), BF16),
            pltpu.VMEM((1, heads, length), F32),
            pltpu.VMEM((2, heads, size, size), BF16),
            pltpu.VMEM((heads, size, size), BF16),
            *[pltpu.VMEM((heads, size, size), F32)] * 2,
            pltpu.VMEM((8, length), F32),
            *[pltpu.VMEM(tile, F32)] * 2,
            *[pltpu.VMEM((heads, length, size), F32)] * 5,
            dma((5,)),
            *[dma((1,))] * 4,
            *[dma((n_far,))] * 4,
            dma((1,)),
            dma((1,)),
            dma((4, heads)),
            dma((4, heads)),
            dma((heads,)),
            dma((heads,)),
            dma((1,)),
            dma((1,)),
            *[dma((heads,))] * 4,
            pltpu.SemaphoreType.REGULAR((n_far,)),
            *[pltpu.SemaphoreType.REGULAR] * 3,
        ],
        compiler_params=pltpu.CompilerParams(
            collective_id=0, has_side_effects=True, vmem_limit_bytes=24 << 20
        ),
    )(
        *(
            pltpu.with_memory_space_constraint(x, pltpu.HBM)
            for x in (queries, keys, values, output_gradient, log_decay)
        )
    )
    return pl.pallas_call(
        put_kernel,
        out_shape=shapes,
        in_specs=[anywhere] * 3,
        out_specs=[anywhere] * 3,
        scratch_shapes=[dma((3,))],
        compiler_params=pltpu.CompilerParams(vmem_limit_bytes=4 << 20),
    )(*results)


def solution(mesh):
    in_specs = (
        P("pipe", "seq", "head"),
        P("pipe", "seq", "head"),
        P("pipe", "seq", "head"),
        P("pipe", "seq", "head"),
        P("pipe", "head", "seq"),
    )
    out_specs = (P("pipe", "seq", "head"), P("pipe", "seq", "head"), P("pipe", "seq", "head"))
    body = functools.partial(per_device, mesh.shape["pipe"], mesh.shape["seq"])
    return jax.shard_map(body, mesh=mesh, in_specs=in_specs, out_specs=out_specs, check_vma=False)
```

```python
import functools

import jax
import jax.numpy as jnp
from jax import lax
from jax.experimental import pallas as pl
from jax.experimental.pallas import tpu as pltpu
from jax.sharding import PartitionSpec as P

MESH = pl.DeviceIdType.MESH
INNER = (((1,), (1,)), ((), ()))
OUTER = (((0,), (0,)), ((), ()))
F32 = jnp.float32
BF16 = jnp.bfloat16


def mm(a, b):
    return jnp.dot(a, b, preferred_element_type=F32)


def mm_nt(a, b):
    return lax.dot_general(a, b, INNER, preferred_element_type=F32)


def mm_tn(a, b):
    return lax.dot_general(a, b, OUTER, preferred_element_type=F32)


def running_sums(ld, part_ref, cum_ref, tot_ref):
    heads, length = ld.shape
    high = ld.astype(BF16).astype(F32)
    rest = ld - high
    middle = rest.astype(BF16).astype(F32)
    part_ref[0:heads, :] = high
    part_ref[heads : 2 * heads, :] = middle
    part_ref[2 * heads : 3 * heads, :] = rest - middle
    earlier = (
        (
            lax.broadcasted_iota(jnp.int32, (length, length), 0)
            <= lax.broadcasted_iota(jnp.int32, (length, length), 1)
        )
        .astype(F32)
        .astype(BF16)
    )
    sums = mm(part_ref[...].astype(BF16), earlier)
    cum_ref[0:heads, :] = sums[0:heads] + sums[heads : 2 * heads] + sums[2 * heads : 3 * heads]
    tot_ref[...] = jnp.broadcast_to(cum_ref[:, length - 1 : length], tot_ref.shape)


def as_columns(cum_ref, h, half):
    blocks = []
    for b in range(2):
        row = cum_ref[h : h + 1, b * half : (b + 1) * half]
        blocks.append(jnp.broadcast_to(row, (half, half)).T)
    return jnp.concatenate(blocks, axis=0)


def weighted_state(x, weights, y):
    return mm((x.T.astype(F32) * weights).astype(BF16), y)


def kernel(
    n_pipe,
    n_chip,
    n_late,
    q_hbm,
    k_hbm,
    v_hbm,
    g_hbm,
    ld_hbm,
    oq_ref,
    ok_ref,
    ov_ref,
    q_ref,
    k_ref,
    v_ref,
    g_ref,
    ld_ref,
    part_ref,
    cum_ref,
    tot_ref,
    tot_sib_ref,
    chip_tot_ref,
    far_tot_ref,
    weight_ref,
    local_ref,
    sib_state_ref,
    agg_ref,
    far_ref,
    ship_ref,
    up_ref,
    up_ld_ref,
    up_state_ref,
    up_sib_state_ref,
    up_local_ref,
    up_sib_local_ref,
    up_cum_ref,
    up_tot_ref,
    up_tot_sib_ref,
    up_lead_ref,
    up_tail_ref,
    iq_ref,
    ik_ref,
    iv_ref,
    in_sem,
    tot_send,
    tot_recv,
    x_send,
    x_recv,
    ft_send,
    ft_recv,
    agg_send,
    agg_recv,
    ld_send,
    ld_recv,
    y_send,
    y_recv,
    st_send,
    st_recv,
    et_send,
    et_recv,
    ex_send,
    ex_recv,
    eu_send,
    eu_recv,
    ready,
    low_ready,
    cross_ready,
    sib_ready,
):
    length, width = q_ref.shape
    heads = ld_ref.shape[1]
    size = width // heads
    half = length // 2
    n_far = n_chip - 1

    pipe = lax.axis_index("pipe")
    seq = lax.axis_index("seq")
    chip = lax.div(seq, 2)
    core = lax.rem(seq, 2)
    sibling = seq + 1 - 2 * core
    step = 2 * core - 1
    n_partner = core * (n_far - chip) + (1 - core) * chip
    below = lax.rem(pipe + n_pipe - 1, n_pipe)
    above = lax.rem(pipe + 1, n_pipe)
    is_source = pipe > 0
    is_target = pipe < n_pipe - 1
    late_states = chip < n_late

    def partner(d):
        return 2 * (chip + step * d) + (1 - core)

    def cols(ref, h):
        return ref[:, h * size : (h + 1) * size]

    def remote(src, dst, send, recv, device):
        return pltpu.make_async_remote_copy(
            src_ref=src,
            dst_ref=dst,
            send_sem=send,
            recv_sem=recv,
            device_id=device,
            device_id_type=MESH,
        )

    def signal(sem, device):
        pl.semaphore_signal(sem, inc=1, device_id=device, device_id_type=MESH)

    inputs = (q_hbm, g_hbm, k_hbm, v_hbm)
    held = (q_ref, g_ref, k_ref, v_ref)

    def tot_copy():
        return remote(tot_ref, tot_sib_ref, tot_send.at[0], tot_recv.at[0], {"seq": sibling})

    def x_copy():
        return remote(
            local_ref.at[core], sib_state_ref, x_send.at[0], x_recv.at[0], {"seq": sibling}
        )

    def tot_far(d):
        return remote(
            chip_tot_ref,
            far_tot_ref.at[d - 1],
            ft_send.at[d - 1],
            ft_recv.at[d - 1],
            {"seq": partner(d)},
        )

    def agg_far(d):
        return remote(
            agg_ref,
            far_ref.at[d - 1],
            agg_send.at[d - 1],
            agg_recv.at[d - 1],
            {"seq": partner(d)},
        )

    def ld_copy():
        return remote(ld_ref, up_ld_ref, ld_send.at[0], ld_recv.at[0], {"pipe": below})

    def y_copy(i, h):
        return remote(
            held[i].at[:, pl.ds(h * size, size)],
            up_ref.at[i, h],
            y_send.at[i, h],
            y_recv.at[i, h],
            {"pipe": below},
        )

    def st_copy(h):
        return remote(
            ship_ref.at[h],
            up_state_ref.at[core, h],
            st_send.at[h],
            st_recv.at[h],
            {"pipe": below},
        )

    def up_tot_copy():
        return remote(up_tot_ref, up_tot_sib_ref, et_send.at[0], et_recv.at[0], {"seq": sibling})

    def up_local_copy(h):
        return remote(
            up_local_ref.at[h], up_sib_local_ref.at[h], ex_send.at[h], ex_recv.at[h], {"seq": sibling}
        )

    def up_state_copy(h):
        return remote(
            up_state_ref.at[core, h],
            up_sib_state_ref.at[h],
            eu_send.at[h],
            eu_recv.at[h],
            {"seq": sibling},
        )

    def ship(some):
        for which, order in ((0, (2, 3, 0, 1)), (1, (0, 1, 2, 3))):

            @pl.when(core == which)
            def _():
                for h in some:
                    for i in order:
                        y_copy(i, h).start()

    barrier = pltpu.get_barrier_semaphore()
    busy = jnp.minimum(pipe, 1)

    @pl.when(is_source)
    def _():
        signal(barrier, {"seq": sibling})

    @pl.when(pipe == 1)
    def _():
        signal(barrier, {"pipe": below})

    @pl.when(jnp.logical_and(is_source, is_target))
    def _():
        signal(barrier, {"pipe": above})

    loads = [pltpu.make_async_copy(ld_hbm, ld_ref, in_sem.at[4])]
    for i, (src, dst) in enumerate(zip(inputs, held)):
        loads.append(pltpu.make_async_copy(src.at[0], dst, in_sem.at[i]))
    @pl.when(is_source)
    def _():
        for load in loads:
            load.start()

    pl.semaphore_wait(barrier, 1 + busy * jnp.minimum(chip, 1) + jnp.minimum(lax.div(pipe, 2), 1))

    @pl.when(jnp.logical_and(is_source, chip < n_far))
    def _():
        signal(barrier, {"seq": seq + 2})

    @pl.when(pipe == 0)
    def _():
        signal(low_ready, {"pipe": above})

    @pl.when(pipe == 1)
    def _():
        pl.semaphore_wait(low_ready, 1)
        signal(cross_ready, {"seq": sibling})

    @pl.when(is_source)
    def _():
        for load in loads:
            load.wait()
        ld_copy().start()
        ship(range(heads - 1))

    last_first = jnp.logical_and(late_states, core == 1)

    @pl.when(jnp.logical_and(is_source, last_first))
    def _():
        ship(range(heads - 1, heads))

    @pl.when(jnp.logical_and(is_source, core == 0))
    def _():
        for d in range(1, n_far + 1):

            @pl.when(d <= n_partner)
            def _():
                signal(ready.at[d - 1], {"seq": partner(d)})

    part_ref[...] = jnp.zeros_like(part_ref)
    cum_ref[...] = jnp.zeros_like(cum_ref)
    up_cum_ref[...] = jnp.zeros_like(up_cum_ref)

    def make_aggregates():
        x_copy().wait_recv()
        for h in range(heads):
            agg_ref[h] = (
                jnp.exp(tot_ref[h : h + 1, :]) * sib_state_ref[h] + local_ref[1 - core, h]
            ).astype(BF16)

    @pl.when(is_source)
    def _():
        running_sums(ld_ref[0], part_ref, cum_ref, tot_ref)
        tot_copy().start()
        lead = jnp.exp(cum_ref[...])
        tail = jnp.exp(tot_ref[:, :1] - cum_ref[...])
        for h in range(heads):
            local_ref[1, h] = weighted_state(cols(q_ref, h), lead[h : h + 1, :], cols(g_ref, h))

        @pl.when(core == 1)
        def _():
            x_copy().start()

        for h in range(heads):
            local_ref[0, h] = weighted_state(cols(k_ref, h), tail[h : h + 1, :], cols(v_ref, h))

        @pl.when(core == 0)
        def _():
            x_copy().start()

        tot_copy().wait_recv()
        chip_tot_ref[...] = tot_ref[...] + tot_sib_ref[...]

        @pl.when(core == 0)
        def _():
            make_aggregates()
            for i in range(n_far):

                @pl.when(i < n_partner)
                def _():
                    d = n_partner - i
                    tot_far(d).start()
                    agg_far(d).start()

    for d in range(1, n_far + 1):

        @pl.when(d > n_partner)
        def _():
            far_ref[d - 1] = jnp.zeros(far_ref.shape[1:], BF16)
            far_tot_ref[d - 1] = jnp.zeros(far_tot_ref.shape[1:], F32)

    at = lax.broadcasted_iota(jnp.int32, (half, half), 0)
    by = lax.broadcasted_iota(jnp.int32, (half, half), 1)
    lower, upper = at >= by, at <= by

    def sibling_part(h):
        if h == 0:
            ld_copy().wait_recv()
            running_sums(up_ld_ref[0], part_ref, up_cum_ref, up_tot_ref)
        row = up_cum_ref[h : h + 1, :]

        @pl.when(core == 0)
        def _():
            y_copy(2, h).wait_recv()
            y_copy(3, h).wait_recv()
            weights = jnp.exp(up_tot_ref[h : h + 1, :1] - row)
            up_local_ref[h] = weighted_state(up_ref[2, h], weights, up_ref[3, h])

        @pl.when(core == 1)
        def _():
            y_copy(0, h).wait_recv()
            y_copy(1, h).wait_recv()
            up_local_ref[h] = weighted_state(up_ref[0, h], jnp.exp(row), up_ref[1, h])

    def inner_part(h):
        col = as_columns(up_cum_ref, h, half)
        up_lead_ref[h] = jnp.exp(col)
        up_tail_ref[h] = jnp.exp(up_tot_ref[h : h + 1, :] - col)
        for which, rest in ((0, (0, 1)), (1, (2, 3))):

            @pl.when(core == which)
            def _():
                for i in rest:
                    y_copy(i, h).wait_recv()

        q, g, k, v = (up_ref[i, h] for i in range(4))
        row0, row1 = up_cum_ref[h : h + 1, :half], up_cum_ref[h : h + 1, half:]
        col0, col1 = col[:half], col[half:]
        d00 = jnp.where(lower, jnp.exp(col0 - row0), 0.0)
        d10 = jnp.exp(col1 - row0)
        d11 = jnp.where(lower, jnp.exp(col1 - row1), 0.0)
        pair0 = (mm_nt(g[:half], v[:half]) * d00).astype(BF16)
        pair1 = (mm_nt(g[half:], v) * jnp.concatenate([d10, d11], axis=1)).astype(BF16)
        iq_ref[h, :half, :] = mm(pair0, k[:half])
        iq_ref[h, half:, :] = mm(pair1, k)
        e00 = jnp.where(upper, jnp.exp(row0 - col0), 0.0)
        e01 = jnp.exp(row1 - col0)
        e11 = jnp.where(upper, jnp.exp(row1 - col1), 0.0)
        e0 = jnp.concatenate([e00, e01], axis=1)
        pair_t0 = (mm_nt(v[:half], g) * e0).astype(BF16)
        pair_t1 = (mm_nt(v[half:], g[half:]) * e11).astype(BF16)
        ik_ref[h, :half, :] = mm(pair_t0, q)
        ik_ref[h, half:, :] = mm(pair_t1, q[half:])
        score_t0 = (mm_nt(k[:half], q) * e0).astype(BF16)
        score_t1 = (mm_nt(k[half:], q[half:]) * e11).astype(BF16)
        iv_ref[h, :half, :] = mm(score_t0, g)
        iv_ref[h, half:, :] = mm(score_t1, g[half:])

    def result(h):
        here = slice(h * size, (h + 1) * size)
        g, k, v = (up_ref[i, h] for i in (1, 2, 3))
        up_local_copy(h).wait_recv()
        up_state_copy(h).wait_recv()
        up_state_ref[1 - core, h] = (
            jnp.exp(up_tot_sib_ref[h : h + 1, :]) * up_sib_state_ref[h].astype(F32)
            + up_sib_local_ref[h]
        ).astype(BF16)
        state_in, state_rev = up_state_ref[0, h], up_state_ref[1, h]
        for b in range(2):
            rows = slice(b * half, (b + 1) * half)
            lead, tail = up_lead_ref[h, rows, :], up_tail_ref[h, rows, :]
            oq_ref[0, rows, here] = (
                iq_ref[h, rows, :] + lead * mm_nt(g[rows], state_in)
            ).astype(BF16)
            ok_ref[0, rows, here] = (
                ik_ref[h, rows, :] + tail * mm_nt(v[rows], state_rev)
            ).astype(BF16)
            ov_ref[0, rows, here] = (iv_ref[h, rows, :] + tail * mm(k[rows], state_rev)).astype(
                BF16
            )

    half_heads = heads // 2

    @pl.when(jnp.logical_and(is_source, core == 1))
    def _():
        make_aggregates()
        for d in range(1, n_far + 1):

            @pl.when(d <= n_partner)
            def _():
                pl.semaphore_wait(ready.at[d - 1], 1)
                tot_far(d).start()
                agg_far(d).start()

    @pl.when(is_target)
    def _():
        for h in range(half_heads):
            sibling_part(h)
            inner_part(h)

    @pl.when(pipe == 1)
    def _():
        pl.semaphore_wait(cross_ready, 1)
        signal(sib_ready, {"pipe": below})

    def middle_heads():
        up_tot_copy().start()
        for h in range(half_heads):
            up_local_copy(h).start()
        for h in range(half_heads, heads - 1):
            sibling_part(h)
            up_local_copy(h).start()
            inner_part(h)

    @pl.when(pipe == 0)
    def _():
        pl.semaphore_wait(sib_ready, 1)

    @pl.when(jnp.logical_and(is_target, last_first))
    def _():
        middle_heads()

    @pl.when(is_source)
    def _():
        between = jnp.zeros(tot_ref.shape, F32)
        for d in range(1, n_far + 1):

            @pl.when(d <= n_partner)
            def _():
                tot_far(d).wait_recv()
                agg_far(d).wait_recv()

            weight_ref[d - 1] = jnp.exp(between)
            between = between + far_tot_ref[d - 1]

        for h in range(heads):
            total = jnp.zeros((size, size), F32)
            for d in range(1, n_far + 1):
                total = total + weight_ref[d - 1, h : h + 1, :] * far_ref[d - 1, h].astype(F32)
            ship_ref[h] = total.astype(BF16)
            st_copy(h).start()

    @pl.when(jnp.logical_and(is_source, jnp.logical_not(last_first)))
    def _():
        ship(range(heads - 1, heads))

    @pl.when(jnp.logical_and(is_target, jnp.logical_not(last_first)))
    def _():
        middle_heads()

    @pl.when(jnp.logical_and(is_target, last_first))
    def _():
        sibling_part(heads - 1)
        up_local_copy(heads - 1).start()
        inner_part(heads - 1)

    @pl.when(is_source)
    def _():
        tot_copy().wait_send()
        x_copy().wait_send()
        for d in range(1, n_far + 1):

            @pl.when(d <= n_partner)
            def _():
                tot_far(d).wait_send()
                agg_far(d).wait_send()

        ld_copy().wait_send()
        for h in range(heads - 1):
            for i in range(4):
                y_copy(i, h).wait_send()

    @pl.when(is_target)
    def _():
        for h in range(heads):
            st_copy(h).wait_recv()
            up_state_copy(h).start()
        up_tot_copy().wait_recv()

    @pl.when(jnp.logical_and(is_target, jnp.logical_not(last_first)))
    def _():
        sibling_part(heads - 1)
        up_local_copy(heads - 1).start()

    @pl.when(jnp.logical_and(is_target, jnp.logical_not(late_states)))
    def _():
        for h in range(heads - 1):
            result(h)

    @pl.when(jnp.logical_and(is_target, jnp.logical_not(last_first)))
    def _():
        inner_part(heads - 1)

    @pl.when(jnp.logical_and(is_target, late_states))
    def _():
        for h in range(heads - 1):
            result(h)

    @pl.when(is_target)
    def _():
        result(heads - 1)
        up_tot_copy().wait_send()
        for h in range(heads):
            up_local_copy(h).wait_send()

    @pl.when(jnp.logical_not(is_target))
    def _():
        for o in (oq_ref, ok_ref, ov_ref):
            o[...] = jnp.zeros_like(o)

    @pl.when(is_target)
    def _():
        for h in range(heads):
            up_state_copy(h).wait_send()

    @pl.when(is_source)
    def _():
        for i in range(4):
            y_copy(i, heads - 1).wait_send()
        for h in range(heads):
            st_copy(h).wait_send()


def put_kernel(a_ref, b_ref, c_ref, oa_ref, ob_ref, oc_ref, sem):
    copies = [
        pltpu.make_async_copy(src, dst, sem.at[i])
        for i, (src, dst) in enumerate(((a_ref, oa_ref), (b_ref, ob_ref), (c_ref, oc_ref)))
    ]
    for copy in copies:
        copy.start()
    for copy in copies:
        copy.wait()


def per_device(n_pipe, n_seq, queries, keys, values, output_gradient, log_decay):
    length, width = queries.shape[1:]
    heads = log_decay.shape[1]
    size = width // heads
    n_chip = n_seq // 2
    n_far = n_chip - 1
    dma = pltpu.SemaphoreType.DMA
    tile = (8, size)
    anywhere = pl.BlockSpec(memory_space=pl.ANY)
    vmem = pl.BlockSpec(memory_space=pltpu.VMEM)
    shapes = [jax.ShapeDtypeStruct(queries.shape, BF16)] * 3
    results = pl.pallas_call(
        functools.partial(kernel, n_pipe, n_chip, n_chip // 2),
        out_shape=shapes,
        in_specs=[pl.BlockSpec(memory_space=pltpu.HBM)] * 5,
        out_specs=[vmem] * 3,
        scratch_shapes=[
            *[pltpu.VMEM((length, width), BF16)] * 4,
            pltpu.VMEM((1, heads, length), F32),
            pltpu.VMEM((16, length), F32),
            pltpu.VMEM((8, length), F32),
            *[pltpu.VMEM(tile, F32)] * 3,
            *[pltpu.VMEM((n_far, *tile), F32)] * 2,
            pltpu.VMEM((2, heads, size, size), F32),
            pltpu.VMEM((heads, size, size), F32),
            pltpu.VMEM((heads, size, size), BF16),
            pltpu.VMEM((n_far, heads, size, size), BF16),
            pltpu.VMEM((heads, size, size), BF16),
            pltpu.VMEM((4, heads, length, size), BF16),
            pltpu.VMEM((1, heads, length), F32),
            pltpu.VMEM((2, heads, size, size), BF16),
            pltpu.VMEM((heads, size, size), BF16),
            *[pltpu.VMEM((heads, size, size), F32)] * 2,
            pltpu.VMEM((8, length), F32),
            *[pltpu.VMEM(tile, F32)] * 2,
            *[pltpu.VMEM((heads, length, size), F32)] * 5,
            dma((5,)),
            *[dma((1,))] * 4,
            *[dma((n_far,))] * 4,
            dma((1,)),
            dma((1,)),
            dma((4, heads)),
            dma((4, heads)),
            dma((heads,)),
            dma((heads,)),
            dma((1,)),
            dma((1,)),
            *[dma((heads,))] * 4,
            pltpu.SemaphoreType.REGULAR((n_far,)),
            *[pltpu.SemaphoreType.REGULAR] * 3,
        ],
        compiler_params=pltpu.CompilerParams(
            collective_id=0, has_side_effects=True, vmem_limit_bytes=24 << 20
        ),
    )(
        *(
            pltpu.with_memory_space_constraint(x, pltpu.HBM)
            for x in (queries, keys, values, output_gradient, log_decay)
        )
    )
    return pl.pallas_call(
        put_kernel,
        out_shape=shapes,
        in_specs=[anywhere] * 3,
        out_specs=[anywhere] * 3,
        scratch_shapes=[dma((3,))],
        compiler_params=pltpu.CompilerParams(vmem_limit_bytes=4 << 20),
    )(*results)


def solution(mesh):
    in_specs = (
        P("pipe", "seq", "head"),
        P("pipe", "seq", "head"),
        P("pipe", "seq", "head"),
        P("pipe", "seq", "head"),
        P("pipe", "head", "seq"),
    )
    out_specs = (P("pipe", "seq", "head"), P("pipe", "seq", "head"), P("pipe", "seq", "head"))
    body = functools.partial(per_device, mesh.shape["pipe"], mesh.shape["seq"])
    return jax.shard_map(body, mesh=mesh, in_specs=in_specs, out_specs=out_specs, check_vma=False)
```
